768 devices in a mesh: slab: 48 (over x_lo, z, core), filt: 16 (over x_hi, y).
Axes of the slice: x: 4 (x_hi: 2, x_lo: 2; x = x_hi * 2 + x_lo), y: 8, z: 12, core: 2. Of those that a mesh axis runs over, the one named last changes fastest.
Arguments:
- volume: bfloat16 [2, 64, 192, 8, 256], P(None, 'filt', 'slab'), may hold values from -6 to 6
- first_weight: bfloat16 [64, 128, 2, 2, 2], P(None, 'filt'), may hold values from -0.25 to 0.25
- second_weight: bfloat16 [128, 128, 3, 3, 3], P(None, 'filt'), may hold values from -0.109375 to 0.109375
- out_grad: bfloat16 [2, 128, 96, 4, 128], P(None, 'filt', 'slab'), may hold values from -0.01953125 to 0.01953125
Outputs:
- result: bfloat16 [2, 128, 96, 4, 128], P(None, 'filt', 'slab')
- weight_one: float32 [64, 128, 2, 2, 2], P(None, 'filt')
- weight_two: float32 [128, 128, 3, 3, 3], P(None, 'filt')
The draws below stay inside these ranges and needn't reach their ends.
All inputs are finite; a program needn't handle non-finite values.
Results may differ from the reference program's by a relative error of at most 0.0054.
Values may be sent and summed in bfloat16 or wider, within the bound.
A program may use at most 64 MiB of HBM per device.

```python
import jax
import jax.numpy as jnp
from jax import lax

VOLUMES = 2
C_IN = 64
MID = 128
HO = 4
WO = 128
DO = 96
DI = 192
HI = 8
WI = 256


def levels(own_key, dims, shards, low, top_value):
    def one(dim, parts):
        steps = jax.random.uniform(jax.random.fold_in(jax.random.fold_in(own_key, 6), dim), (parts,), jnp.float32, low / len(shards), top_value / len(shards))
        return jnp.repeat(jnp.exp(steps), dims[dim] // parts).reshape((-1,) + (1,) * (len(dims) - dim - 1))

    factor_of = one(*shards[0])
    for cut in shards[1:]:
        factor_of = factor_of * one(*cut)
    return factor_of


def normal_values(own_key, extent, deviation, limit, pieces=(), dtype=jnp.bfloat16):
    drawn = deviation * jax.random.normal(own_key, extent, jnp.float32)
    if pieces:
        drawn = drawn * levels(own_key, extent, pieces, -0.22, 0.18)
    return jnp.clip(drawn, -limit, limit).astype(dtype)


def setup_inputs(seed: int = 0) -> dict:
    key_of = jax.random.split(jax.random.key(seed), 5)
    volume = normal_values(key_of[0], (VOLUMES, C_IN, DI, HI, WI), 1.0, 6.0, ((1, 16), (2, 48)))
    first_weight = normal_values(key_of[1], (C_IN, MID, 2, 2, 2), (C_IN * 8) ** -0.5, 0.25, ((1, 16),))
    second_weight = normal_values(key_of[2], (MID, MID, 3, 3, 3), (MID * 27) ** -0.5, 0.109375, ((1, 16),))
    out_grad = normal_values(key_of[3], (VOLUMES, MID, DO, HO, WO), ((VOLUMES * DO * HO * WO) ** -0.5), 0.01953125, ((1, 16), (2, 48)))
    return {"volume": volume, "first_weight": first_weight, "second_weight": second_weight, "out_grad": out_grad}


def silu_value(values):
    return values * jax.nn.sigmoid(values)


def silu_slope(values):
    logistic = jax.nn.sigmoid(values)
    return logistic * (1.0 + values * (1.0 - logistic))


def reference(volume, first_weight, second_weight, out_grad):
    highest = lax.Precision.HIGHEST
    inputs = volume.astype(jnp.float32)
    first_pre = lax.conv_general_dilated(inputs, first_weight.astype(jnp.float32), (2, 2, 2), "VALID", dimension_numbers=("NCDHW", "IODHW", "NCDHW"), precision=highest, preferred_element_type=jnp.float32)
    hidden = silu_value(first_pre).astype(jnp.bfloat16)
    hidden_wide = hidden.astype(jnp.float32)
    kernel = second_weight.astype(jnp.float32)
    same_pad = ((1, 1), (1, 1), (1, 1))
    second_pre = lax.conv_general_dilated(hidden_wide, kernel, (1, 1, 1), same_pad, dimension_numbers=("NCDHW", "IODHW", "NCDHW"), precision=highest, preferred_element_type=jnp.float32)
    result = silu_value(second_pre).astype(jnp.bfloat16)
    second_grad = (out_grad.astype(jnp.float32) * silu_slope(second_pre)).astype(jnp.bfloat16)
    grad_wide = second_grad.astype(jnp.float32)
    flipped = kernel[:, :, ::-1, ::-1, ::-1]
    mid_grad = lax.conv_general_dilated(grad_wide, flipped, (1, 1, 1), same_pad, dimension_numbers=("NCDHW", "OIDHW", "NCDHW"), precision=highest, preferred_element_type=jnp.float32)
    first_grad = (mid_grad * silu_slope(first_pre)).astype(jnp.bfloat16)
    hidden_pad = jnp.pad(hidden_wide, ((0, 0), (0, 0), (1, 1), (1, 1), (1, 1)))
    weight_two = lax.conv_general_dilated(hidden_pad, grad_wide, (1, 1, 1), "VALID", dimension_numbers=("CNDHW", "IODHW", "NCDHW"), precision=highest, preferred_element_type=jnp.float32)
    weight_one = lax.conv_general_dilated(inputs, first_grad.astype(jnp.float32), (1, 1, 1), "VALID", rhs_dilation=(2, 2, 2), dimension_numbers=("CNDHW", "IODHW", "NCDHW"), precision=highest, preferred_element_type=jnp.float32)
    return result, weight_one, weight_two
```

```python
import functools

import jax
import jax.numpy as jnp
from jax import lax
from jax.experimental import pallas as pl
from jax.experimental.pallas import tpu as pltpu
from jax.sharding import PartitionSpec as P

BF = jnp.bfloat16
F32 = jnp.float32
MESH = pl.DeviceIdType.MESH
VMEM = pl.BlockSpec(memory_space=pltpu.VMEM)


def silu_value(values):
    return values * jax.nn.sigmoid(values)


def silu_slope(values):
    logistic = jax.nn.sigmoid(values)
    return logistic * (1.0 + values * (1.0 - logistic))


def exchange_kernel(axis, n, kinds, *refs):
    count = len(kinds)
    ins, outs = refs[:count], refs[count : 2 * count]
    send_sem, recv_sem, own_sem = refs[2 * count :]
    me = lax.axis_index(axis)
    barrier = pltpu.get_barrier_semaphore()

    def greet(r, carry):
        pl.semaphore_signal(
            barrier, inc=1, device_id={axis: lax.rem(me + r, n)}, device_id_type=MESH
        )
        return carry

    lax.fori_loop(1, n, greet, 0)
    pl.semaphore_wait(barrier, n - 1)

    def copy(i, r):
        to = lax.rem(me + r, n)
        source = ins[i].at[to] if kinds[i] else ins[i]
        return pltpu.make_async_remote_copy(
            src_ref=source,
            dst_ref=outs[i].at[me],
            send_sem=send_sem.at[i, r],
            recv_sem=recv_sem.at[i, r],
            device_id={axis: to},
            device_id_type=MESH,
        )

    def start(r, carry):
        for i in range(count):
            copy(i, r).start()
        return carry

    lax.fori_loop(1, n, start, 0)
    own = [
        pltpu.make_async_copy(
            ins[i].at[me] if kinds[i] else ins[i], outs[i].at[me], own_sem.at[i]
        )
        for i in range(count)
    ]
    for one in own:
        one.start()
    for one in own:
        one.wait()

    def finish(r, carry):
        for i in range(count):
            copy(i, r).wait()
        return carry

    lax.fori_loop(1, n, finish, 0)


def exchange(axis, arrays, kinds, number, name):
    n = lax.axis_size(axis)
    count = len(arrays)
    shapes = [
        jax.ShapeDtypeStruct(a.shape if kind else (n,) + a.shape, a.dtype)
        for a, kind in zip(arrays, kinds)
    ]
    return pl.pallas_call(
        functools.partial(exchange_kernel, axis, n, kinds),
        out_shape=shapes,
        in_specs=[VMEM] * count,
        out_specs=[VMEM] * count,
        scratch_shapes=[
            pltpu.SemaphoreType.DMA((count, n)),
            pltpu.SemaphoreType.DMA((count, n)),
            pltpu.SemaphoreType.DMA((count,)),
        ],
        compiler_params=pltpu.CompilerParams(
            collective_id=number, has_side_effects=True
        ),
        name=name,
    )(*arrays)


def halo_kernel(axis, n, up_ref, down_ref, below_ref, above_ref, send_sem, recv_sem):
    me = lax.axis_index(axis)
    after, before = lax.rem(me + 1, n), lax.rem(me + n - 1, n)
    barrier = pltpu.get_barrier_semaphore()
    for peer in (before, after):
        pl.semaphore_signal(
            barrier, inc=1, device_id={axis: peer}, device_id_type=MESH
        )
    pl.semaphore_wait(barrier, 2)
    copies = [
        pltpu.make_async_remote_copy(
            src_ref=source,
            dst_ref=target,
            send_sem=send_sem.at[i],
            recv_sem=recv_sem.at[i],
            device_id={axis: peer},
            device_id_type=MESH,
        )
        for i, (source, target, peer) in enumerate(
            ((up_ref, below_ref, after), (down_ref, above_ref, before))
        )
    ]
    for one in copies:
        one.start()
    for one in copies:
        one.wait()


def halo(axis, up, down, number, name):
    n = lax.axis_size(axis)
    return pl.pallas_call(
        functools.partial(halo_kernel, axis, n),
        out_shape=[jax.ShapeDtypeStruct(a.shape, a.dtype) for a in (up, down)],
        in_specs=[VMEM] * 2,
        out_specs=[VMEM] * 2,
        scratch_shapes=[
            pltpu.SemaphoreType.DMA((2,)),
            pltpu.SemaphoreType.DMA((2,)),
        ],
        compiler_params=pltpu.CompilerParams(
            collective_id=number, has_side_effects=True
        ),
        name=name,
    )(up, down)


def compute(kernel, shapes, arrays, name, scratch=(), scalar=None):
    specs = [VMEM] * len(arrays)
    if scalar is not None:
        arrays = [scalar] + list(arrays)
        specs = [pl.BlockSpec(memory_space=pltpu.SMEM)] + specs
    return pl.pallas_call(
        kernel,
        out_shape=[jax.ShapeDtypeStruct(s, d) for s, d in shapes],
        in_specs=specs,
        out_specs=[VMEM] * len(shapes),
        scratch_shapes=list(scratch),
        name=name,
    )(*arrays)


def one_hot(source_of_row, size):
    row = lax.broadcasted_iota(jnp.int32, (size, size), 0)
    column = lax.broadcasted_iota(jnp.int32, (size, size), 1)
    return jnp.where(source_of_row(row) == column, 1.0, 0.0).astype(BF)


def pieces_kernel(x_ref, out_ref):
    def source(o):
        b, d, h = o >> 7, (o >> 6) & 1, (o >> 4) & 3
        c, i, j = (o >> 2) & 3, (o >> 1) & 1, o & 1
        return (b << 7) + (c << 5) + ((2 * d + i) << 3) + 2 * h + j

    rows = one_hot(source, 256)
    row = lax.broadcasted_iota(jnp.int32, (256, 256), 0)
    column = lax.broadcasted_iota(jnp.int32, (256, 256), 1)
    columns = jnp.where(row == 2 * (column & 127) + (column >> 7), 1.0, 0.0).astype(BF)
    half = jnp.dot(rows, x_ref[...], preferred_element_type=F32).astype(BF)
    out_ref[...] = jnp.dot(half, columns, preferred_element_type=F32).astype(BF)


def first_kernel(x_ref, w_ref, pre_ref, hidden_ref):
    pre = jnp.dot(w_ref[:, :256], x_ref[:, :128], preferred_element_type=F32)
    pre += jnp.dot(w_ref[:, 256:], x_ref[:, 128:], preferred_element_type=F32)
    pre_ref[...] = pre
    hidden_ref[...] = silu_value(pre).astype(BF)


def shifted(values, by):
    if by == 0:
        return values
    lane = lax.broadcasted_iota(jnp.int32, values.shape, 1)
    rolled = pltpu.roll(values, (-by) % 128, 1)
    return jnp.where(lane == (127 if by > 0 else 0), 0.0, rolled)


def tap(a, e, g):
    return ((a * 3 + e) * 3 + g) * 8


def second_kernel(hidden_ref, w_ref, own_ref, up_ref, down_ref, y_ref):
    for q in range(16):
        y_ref[q] = jnp.dot(w_ref[...], hidden_ref[q], preferred_element_type=F32)
    for b in range(2):
        for d in range(-1, 3):
            for h in range(4):
                total = None
                for g in range(3):
                    part = None
                    for a in range(3):
                        plane = d + a - 1
                        if plane < 0 or plane > 1:
                            continue
                        for e in range(3):
                            row = h + e - 1
                            if row < 0 or row > 3:
                                continue
                            at = tap(a, e, g)
                            term = y_ref[b * 8 + plane * 4 + row, at : at + 8, :]
                            part = term if part is None else part + term
                    part = shifted(part, g - 1)
                    total = part if total is None else total + part
                if d < 0:
                    down_ref[b * 4 + h] = total
                elif d > 1:
                    up_ref[b * 4 + h] = total
                else:
                    own_ref[b * 8 + d * 4 + h] = total


def result_kernel(
    edge_ref, own_ref, below_ref, above_ref, grad_ref, result_ref, sg_ref, up_ref, down_ref
):
    low, high = edge_ref[0] > 0, edge_ref[1] > 0
    for b in range(2):
        for d in range(2):
            for h in range(4):
                q, r = b * 8 + d * 4 + h, b * 4 + h
                other = below_ref[r] if d == 0 else above_ref[r]
                pre = own_ref[q] + jnp.where(low if d == 0 else high, other, 0.0)
                result_ref[q] = silu_value(pre).astype(BF)
                grad = (grad_ref[q].astype(F32) * silu_slope(pre)).astype(BF)
                sg_ref[q] = grad
                if d == 0:
                    down_ref[r] = grad
                else:
                    up_ref[r] = grad


def back_kernel(
    edge_ref, sg_ref, below_ref, above_ref, w_ref, hidden_ref, mid_ref, w2_ref, s_ref
):
    low, high = edge_ref[0] > 0, edge_ref[1] > 0
    total = None
    for b in range(2):
        views = {}
        for plane in range(-1, 3):
            for h in range(4):
                if plane < 0:
                    value = jnp.where(low, below_ref[b * 4 + h].astype(F32), 0.0)
                elif plane > 1:
                    value = jnp.where(high, above_ref[b * 4 + h].astype(F32), 0.0)
                else:
                    value = sg_ref[b * 8 + plane * 4 + h].astype(F32)
                for g in range(3):
                    views[plane, h, g] = shifted(value, 1 - g)
        for d in range(2):
            for h in range(4):
                q = b * 8 + d * 4 + h
                for a in range(3):
                    for e in range(3):
                        row = h - e + 1
                        for g in range(3):
                            at = tap(a, e, g)
                            if row < 0 or row > 3:
                                block = jnp.zeros((8, 128), F32)
                            else:
                                block = views[d - a + 1, row, g]
                            s_ref[q, at : at + 8, :] = block
    for q in range(16):
        taps = s_ref[q].astype(BF)
        mid_ref[q] = jnp.dot(w_ref[...], taps, preferred_element_type=F32).astype(BF)
        part = lax.dot_general(
            taps, hidden_ref[q], (((1,), (1,)), ((), ())), preferred_element_type=F32
        )
        total = part if total is None else total + part
    w2_ref[...] = total


def first_back_kernel(parts_ref, pre_ref, x_ref, w1_ref):
    mid = parts_ref[0].astype(F32)
    for p in range(1, 16):
        mid += parts_ref[p].astype(F32)
    grad = (mid * silu_slope(pre_ref[...])).astype(BF)
    for k in range(2):
        w1_ref[:, k * 256 : (k + 1) * 256] = lax.dot_general(
            grad,
            x_ref[:, k * 128 : (k + 1) * 128],
            (((1,), (1,)), ((), ())),
            preferred_element_type=F32,
        )


def sum_kernel(parts_ref, out_ref):
    total = parts_ref[0]
    for p in range(1, parts_ref.shape[0]):
        total += parts_ref[p]
    out_ref[...] = total


def sum_blocks(parts, name):
    return compute(sum_kernel, [(parts.shape[1:], parts.dtype)], [parts], name)[0]


def on_device(volume, first_weight, second_weight, out_grad):
    slabs = lax.axis_size("slab")
    me = lax.axis_index("slab")
    edge = jnp.stack([me > 0, me < slabs - 1]).astype(jnp.int32)
    w_one = first_weight.transpose(1, 4, 0, 2, 3).reshape(8, 512)
    w_two = second_weight.transpose(2, 3, 4, 1, 0).reshape(216, 128)
    w_two_t = second_weight.transpose(0, 2, 3, 4, 1).reshape(128, 216)
    grad_rows = out_grad.transpose(0, 2, 3, 1, 4).reshape(16, 8, 128)

    (pieces,) = compute(
        pieces_kernel, [((256, 256), BF)], [volume.reshape(256, 256)], "pieces"
    )
    x_all, w_all = exchange(
        "filt", [pieces.reshape(16, 16, 256), w_one], (1, 0), 1, "send_volume"
    )
    x_all, w_all = x_all.reshape(256, 256), w_all.reshape(128, 512)
    pre, hidden_own = compute(
        first_kernel, [((128, 128), F32), ((128, 128), BF)], [x_all, w_all], "first"
    )
    (hidden,) = exchange("filt", [hidden_own], (0,), 2, "send_hidden")
    own, up, down = compute(
        second_kernel,
        [((16, 8, 128), F32), ((8, 8, 128), F32), ((8, 8, 128), F32)],
        [hidden, w_two],
        "second",
        scratch=[pltpu.VMEM((16, 216, 128), F32)],
    )
    below, above = halo("slab", up, down, 3, "send_rims")
    result, sg, up, down = compute(
        result_kernel,
        [((16, 8, 128), BF), ((16, 8, 128), BF), ((8, 8, 128), BF), ((8, 8, 128), BF)],
        [own, below, above, grad_rows],
        "result",
        scalar=edge,
    )
    below, above = halo("slab", up, down, 4, "send_grad_rims")
    mid, w2_part = compute(
        back_kernel,
        [((16, 128, 128), BF), ((216, 128), F32)],
        [sg, below, above, w_two_t, hidden],
        "back",
        scratch=[pltpu.VMEM((16, 216, 128), F32)],
        scalar=edge,
    )
    (mid_parts,) = exchange("filt", [mid], (1,), 5, "send_mid")
    (w1_part,) = compute(
        first_back_kernel, [((128, 512), F32)], [mid_parts, pre, x_all], "first_back"
    )
    (w1_parts,) = exchange("filt", [w1_part.reshape(16, 8, 512)], (1,), 6, "send_w1")
    w1_own = sum_blocks(w1_parts, "sum_w1")

    rows = jnp.concatenate([w2_part, w1_own.reshape(32, 128)], axis=0)
    blocks = -(-rows.shape[0] // (8 * slabs)) * slabs
    rows = jnp.pad(rows, ((0, blocks * 8 - rows.shape[0]), (0, 0)))
    per = blocks * 8 // slabs
    (parts,) = exchange("slab", [rows.reshape(slabs, per, 128)], (1,), 7, "scatter")
    summed = sum_blocks(parts, "sum_slabs")
    (rows,) = exchange("slab", [summed], (0,), 8, "gather")
    rows = rows.reshape(blocks * 8, 128)
    weight_two = rows[:216].reshape(3, 3, 3, 8, 128).transpose(4, 3, 0, 1, 2)
    weight_one = rows[216:248].reshape(8, 2, 64, 2, 2).transpose(2, 0, 3, 4, 1)
    result = result.reshape(2, 2, 4, 8, 128).transpose(0, 3, 1, 2, 4)
    return (result, weight_one, weight_two)


def solution(mesh):
    in_specs = (
        P(None, "filt", "slab", None, None),
        P(None, "filt", None, None, None),
        P(None, "filt", None, None, None),
        P(None, "filt", "slab", None, None),
    )
    out_specs = (
        P(None, "filt", "slab", None, None),
        P(None, "filt", None, None, None),
        P(None, "filt", None, None, None),
    )
    return jax.shard_map(
        on_device, mesh=mesh, in_specs=in_specs, out_specs=out_specs, check_vma=False
    )
```

```python
import functools

import jax
import jax.numpy as jnp
from jax import lax
from jax.experimental import pallas as pl
from jax.experimental.pallas import tpu as pltpu
from jax.sharding import PartitionSpec as P

BF = jnp.bfloat16
F32 = jnp.float32
MESH = pl.DeviceIdType.MESH
VMEM = pl.BlockSpec(memory_space=pltpu.VMEM)
TAPS = 27
W1_BLOCKS = 4


def silu_value(values):
    return values * jax.nn.sigmoid(values)


def silu_slope(values):
    logistic = jax.nn.sigmoid(values)
    return logistic * (1.0 + values * (1.0 - logistic))


def one_hot(source_of_row, size):
    row = lax.broadcasted_iota(jnp.int32, (size, size), 0)
    column = lax.broadcasted_iota(jnp.int32, (size, size), 1)
    return jnp.where(source_of_row(row) == column, 1.0, 0.0).astype(BF)


def piece_matrices():
    def source(o):
        b, d, h = o >> 7, (o >> 6) & 1, (o >> 4) & 3
        c, i, j = (o >> 2) & 3, (o >> 1) & 1, o & 1
        return (b << 7) + (c << 5) + ((2 * d + i) << 3) + 2 * h + j

    row = lax.broadcasted_iota(jnp.int32, (256, 256), 0)
    column = lax.broadcasted_iota(jnp.int32, (256, 256), 1)
    columns = jnp.where(row == 2 * (column & 127) + (column >> 7), 1.0, 0.0).astype(BF)
    return one_hot(source, 256), columns


def shifted(values, by):
    if by == 0:
        return values
    flat = values.reshape(-1, 128)
    lane = lax.broadcasted_iota(jnp.int32, flat.shape, 1)
    rolled = pltpu.roll(flat, (-by) % 128, 1)
    return jnp.where(lane == (127 if by > 0 else 0), 0.0, rolled).reshape(values.shape)


def tap(a, e, g):
    return ((a * 3 + e) * 3 + g) * 8


def nt_dot(a, b):
    return lax.dot_general(a, b, (((1,), (1,)), ((), ())), preferred_element_type=F32)


def remote(source, target, send, recv, axis, to):
    return pltpu.make_async_remote_copy(
        src_ref=source,
        dst_ref=target,
        send_sem=send,
        recv_sem=recv,
        device_id={axis: to},
        device_id_type=MESH,
    )


def repeat(low, high, step):
    lax.fori_loop(low, high, lambda i, carry: (step(i), carry)[1], 0)


class Scatter:
    def __init__(self, n, me, first, count, blocks, landing, total, out, sems):
        self.n, self.me, self.first = n, me, first
        self.owners, self.per = count
        self.blocks, self.landing, self.total, self.out = blocks, landing, total, out
        self.send_a, self.recv_a, self.send_b, self.recv_b = sems

    def owner(self, j):
        return lax.rem(self.first + j, self.n)

    def index(self):
        return lax.rem(self.me - self.first + self.n, self.n)

    def out_copy(self, j):
        return remote(
            self.blocks.at[pl.ds(j * self.per, self.per)],
            self.landing.at[self.me],
            self.send_a.at[j],
            self.recv_a.at[self.me],
            "slab",
            self.owner(j),
        )

    def in_copy(self, source):
        return remote(
            self.total,
            self.landing.at[source],
            self.send_a.at[0],
            self.recv_a.at[source],
            "slab",
            source,
        )

    def back_copy(self, r):
        at = self.index() * self.per
        return remote(
            self.total,
            self.out.at[pl.ds(at, self.per)],
            self.send_b.at[r],
            self.recv_b.at[self.index()],
            "slab",
            lax.rem(self.me + r, self.n),
        )

    def each_owner(self, step):
        def one(j):
            @pl.when(self.owner(j) != self.me)
            def _():
                step(j)

        repeat(0, self.owners, one)

    def start(self):
        self.each_owner(lambda j: self.out_copy(j).start())

    def reduce(self):
        @pl.when(self.index() < self.owners)
        def _():
            at = pl.ds(self.index() * self.per, self.per)

            def add(r, total):
                source = lax.rem(self.me + self.n - r, self.n)
                self.in_copy(source).wait_recv()
                return total + self.landing[source]

            total = lax.fori_loop(1, self.n, add, self.blocks[at])
            self.total[...] = total
            self.out[at] = total
            repeat(1, self.n, lambda r: self.back_copy(r).start())

    def finish(self):
        def arrive(j):
            remote(
                self.total,
                self.out.at[pl.ds(j * self.per, self.per)],
                self.send_b.at[0],
                self.recv_b.at[j],
                "slab",
                self.owner(j),
            ).wait_recv()

        self.each_owner(arrive)
        self.each_owner(lambda j: self.out_copy(j).wait_send())

        @pl.when(self.index() < self.owners)
        def _():
            repeat(1, self.n, lambda r: self.back_copy(r).wait_send())


def level_kernel(
    filts, slabs, two_count, one_count,
    x_ref, w1_ref, w2_ref, og_ref,
    result_ref, two_out, one_out,
    piece, x_all, w_all, hid, y, own, up, down, below, above,
    sg, sg_below, sg_above, view, s, mid, mid_in, dw1, dw1_in, w2_t, pre_ref,
    two, two_in, two_sum, one, one_in, one_sum,
    fs, fr, hs, hr, ts_a, tr_a, ts_b, tr_b, os_a, or_a, os_b, or_b,
):
    f, z = lax.axis_index("filt"), lax.axis_index("slab")
    barrier = pltpu.get_barrier_semaphore()

    def greet(axis, me, n):
        def one_peer(r):
            pl.semaphore_signal(
                barrier,
                inc=1,
                device_id={axis: lax.rem(me + r, n)},
                device_id_type=MESH,
            )

        repeat(1, n, one_peer)

    greet("filt", f, filts)
    greet("slab", z, slabs)

    def peer(r):
        return lax.rem(f + r, filts)

    def source(r):
        return lax.rem(f + filts - r, filts)

    def filt(i, r, block, target):
        return remote(block, target, fs.at[i, r], fr.at[i, r], "filt", peer(r))

    def to_all(step):
        repeat(1, filts, step)

    rows, columns = piece_matrices()
    half = jnp.dot(rows, x_ref[...], preferred_element_type=F32).astype(BF)
    cut = jnp.dot(half, columns, preferred_element_type=F32).astype(BF)
    piece[...] = cut.reshape(piece.shape)
    x_all[f] = piece[f]
    w_all[f] = w1_ref[...]
    pl.semaphore_wait(barrier, filts + slabs - 2)

    def send_x(r):
        filt(0, r, piece.at[peer(r)], x_all.at[f]).start()
        filt(1, r, w1_ref, w_all.at[f]).start()

    to_all(send_x)
    eye = one_hot(lambda o: o, 128)
    w2_t[...] = nt_dot(eye, w2_ref[...]).astype(BF)
    y[:, :, 0] = jnp.zeros((2, 2, 216, 128), F32)
    y[:, :, 5] = jnp.zeros((2, 2, 216, 128), F32)
    view[:, :, :, 0] = jnp.zeros((3, 2, 4, 8, 128), F32)
    view[:, :, :, 5] = jnp.zeros((3, 2, 4, 8, 128), F32)

    def get_x(r):
        filt(0, r, piece.at[peer(r)], x_all.at[source(r)]).wait_recv()
        filt(1, r, w1_ref, w_all.at[source(r)]).wait_recv()

    to_all(get_x)
    x = x_all[...].reshape(256, 256)
    w = w_all[...].reshape(128, 512)
    pre = jnp.dot(w[:, :256], x[:, :128], preferred_element_type=F32)
    pre += jnp.dot(w[:, 256:], x[:, 128:], preferred_element_type=F32)
    pre_ref[...] = pre
    hid[f] = silu_value(pre).astype(BF)
    to_all(lambda r: filt(2, r, hid.at[f], hid.at[f]).start())

    def spread(q):
        b, d, h = lax.div(q, 8), lax.rem(lax.div(q, 4), 2), lax.rem(q, 4)
        y[b, d, h + 1] = jnp.dot(w2_ref[...], hid[q], preferred_element_type=F32)

    spread(f)

    def get_hidden(r):
        filt(2, r, hid.at[f], hid.at[source(r)]).wait_recv()
        spread(source(r))

    to_all(get_hidden)
    for d in (-1, 2, 0, 1):
        total = None
        for g in range(3):
            part = None
            for a in range(3):
                plane = d + a - 1
                if plane < 0 or plane > 1:
                    continue
                for e in range(3):
                    at = tap(a, e, g)
                    term = y[:, plane, e : e + 4, at : at + 8, :]
                    part = term if part is None else part + term
            part = shifted(part, g - 1)
            total = part if total is None else total + part
        if d < 0:
            down[...] = total
        elif d > 1:
            up[...] = total
        else:
            own[d] = total

    after, before = lax.rem(z + 1, slabs), lax.rem(z + slabs - 1, slabs)

    def rims(i, block_up, block_down, from_below, from_above):
        return (
            remote(block_up, from_below, hs.at[i], hr.at[i], "slab", after),
            remote(block_down, from_above, hs.at[i + 1], hr.at[i + 1], "slab", before),
        )

    first_rims = rims(0, up, down, below, above)
    for copy in first_rims:
        copy.start()
    inside = (z > 0, z < slabs - 1)
    for copy in first_rims:
        copy.wait_recv()
    for d in range(2):
        rim = (below if d == 0 else above)[...]
        second_pre = own[d] + jnp.where(inside[d], rim, 0.0)
        result_ref[:, d] = silu_value(second_pre).astype(BF)
        grad = og_ref[:, d].astype(F32) * silu_slope(second_pre)
        sg[d] = grad.astype(BF)
    second_rims = rims(2, sg.at[1], sg.at[0], sg_below, sg_above)
    for copy in second_rims:
        copy.start()

    def put_view(plane, values):
        for g in range(3):
            view[g, :, plane + 1, 1:5] = shifted(values, 1 - g)

    for d in range(2):
        put_view(d, sg[d].astype(F32))
    for copy in second_rims:
        copy.wait_recv()
    put_view(-1, jnp.where(inside[0], sg_below[...].astype(F32), 0.0))
    put_view(2, jnp.where(inside[1], sg_above[...].astype(F32), 0.0))
    for d in range(2):
        for a in range(3):
            for e in range(3):
                for g in range(3):
                    at = tap(a, e, g)
                    s[:, d, :, at : at + 8, :] = view[g, :, d - a + 2, 2 - e : 6 - e]

    def back(q, total):
        b, d, h = lax.div(q, 8), lax.rem(lax.div(q, 4), 2), lax.rem(q, 4)
        taps = s[b, d, h].astype(BF)
        mid[q] = jnp.dot(w2_t[...], taps, preferred_element_type=F32).astype(BF)
        return total + nt_dot(taps, hid[q])

    total = lax.fori_loop(0, 16, back, jnp.zeros((216, 128), F32))
    to_all(lambda r: filt(3, r, mid.at[peer(r)], mid_in.at[f]).start())
    two[:TAPS] = total.reshape(TAPS, 8, 128)
    two_sums = Scatter(
        slabs, z, 0, two_count, two, two_in, two_sum, two_out, (ts_a, tr_a, ts_b, tr_b)
    )
    two_sums.start()

    def get_mid(r, total):
        filt(3, r, mid.at[peer(r)], mid_in.at[source(r)]).wait_recv()
        return total + mid_in[source(r)].astype(F32)

    mid_grad = lax.fori_loop(1, filts, get_mid, mid[f].astype(F32))
    grad = (mid_grad * silu_slope(pre_ref[...])).astype(BF)
    x = x_all[...].reshape(256, 256)
    for k in range(2):
        part = nt_dot(grad, x[:, k * 128 : (k + 1) * 128])
        dw1[:, :, k * 256 : (k + 1) * 256] = part.reshape(16, 8, 256)
    to_all(lambda r: filt(4, r, dw1.at[peer(r)], dw1_in.at[f]).start())
    two_sums.reduce()

    def get_one(r, total):
        filt(4, r, dw1.at[peer(r)], dw1_in.at[source(r)]).wait_recv()
        return total + dw1_in[source(r)]

    first = lax.fori_loop(1, filts, get_one, dw1[f])
    for j in range(W1_BLOCKS):
        one[j] = first[:, j * 128 : (j + 1) * 128]
    one_first = TAPS if slabs >= TAPS + W1_BLOCKS else 0
    one_sums = Scatter(
        slabs, z, one_first, one_count, one, one_in, one_sum, one_out,
        (os_a, or_a, os_b, or_b),
    )
    one_sums.start()
    one_sums.reduce()
    two_sums.finish()
    one_sums.finish()

    def sent(r):
        filt(0, r, piece.at[peer(r)], x_all.at[f]).wait_send()
        filt(1, r, w1_ref, w_all.at[f]).wait_send()
        filt(2, r, hid.at[f], hid.at[f]).wait_send()
        filt(3, r, mid.at[peer(r)], mid_in.at[f]).wait_send()
        filt(4, r, dw1.at[peer(r)], dw1_in.at[f]).wait_send()

    to_all(sent)
    for copy in first_rims + second_rims:
        copy.wait_send()


def owners(blocks, n):
    per = -(-blocks // n)
    return -(-blocks // per), per


def level(x, w1, w2, og):
    filts, slabs = lax.axis_size("filt"), lax.axis_size("slab")
    two_count, one_count = owners(TAPS, slabs), owners(W1_BLOCKS, slabs)
    two_size, one_size = (c[0] * c[1] for c in (two_count, one_count))
    sem = pltpu.SemaphoreType.DMA
    buffers = [
        ((16, 16, 256), BF), ((16, 16, 256), BF), ((16, 8, 512), BF),
        ((16, 128, 128), BF), ((2, 2, 6, 216, 128), F32), ((2, 2, 4, 8, 128), F32),
        ((2, 4, 8, 128), F32), ((2, 4, 8, 128), F32),
        ((2, 4, 8, 128), F32), ((2, 4, 8, 128), F32),
        ((2, 2, 4, 8, 128), BF), ((2, 4, 8, 128), BF), ((2, 4, 8, 128), BF),
        ((3, 2, 4, 6, 8, 128), F32), ((2, 2, 4, 216, 128), F32),
        ((16, 128, 128), BF), ((16, 128, 128), BF),
        ((16, 8, 512), F32), ((16, 8, 512), F32), ((128, 216), BF), ((128, 128), F32),
        ((two_size, 8, 128), F32), ((slabs, two_count[1], 8, 128), F32),
        ((two_count[1], 8, 128), F32),
        ((one_size, 8, 128), F32), ((slabs, one_count[1], 8, 128), F32),
        ((one_count[1], 8, 128), F32),
    ]
    return pl.pallas_call(
        functools.partial(level_kernel, filts, slabs, two_count, one_count),
        out_shape=[
            jax.ShapeDtypeStruct((2, 2, 4, 8, 128), BF),
            jax.ShapeDtypeStruct((two_size, 8, 128), F32),
            jax.ShapeDtypeStruct((one_size, 8, 128), F32),
        ],
        in_specs=[VMEM] * 4,
        out_specs=[VMEM] * 3,
        scratch_shapes=[pltpu.VMEM(shape, dtype) for shape, dtype in buffers]
        + [
            sem((5, filts)), sem((5, filts)), sem((4,)), sem((4,)),
            sem((two_count[0],)), sem((slabs,)), sem((slabs,)), sem((two_count[0],)),
            sem((one_count[0],)), sem((slabs,)), sem((slabs,)), sem((one_count[0],)),
        ],
        compiler_params=pltpu.CompilerParams(collective_id=1, has_side_effects=True),
        name="level",
    )(x, w1, w2, og)


def on_device(volume, first_weight, second_weight, out_grad):
    w1 = first_weight.transpose(1, 4, 0, 2, 3).reshape(8, 512)
    w2 = second_weight.transpose(2, 3, 4, 1, 0).reshape(216, 128)
    og = out_grad.transpose(0, 2, 3, 1, 4)
    result, two, one = level(volume.reshape(256, 256), w1, w2, og)
    weight_two = two[:TAPS].reshape(3, 3, 3, 8, 128).transpose(4, 3, 0, 1, 2)
    one = one.reshape(2, 2, 8, 32, 2, 2).transpose(1, 3, 2, 4, 5, 0)
    weight_one = one.reshape(64, 8, 2, 2, 2)
    return (result.transpose(0, 3, 1, 2, 4), weight_one, weight_two)


def solution(mesh):
    in_specs = (
        P(None, "filt", "slab", None, None),
        P(None, "filt", None, None, None),
        P(None, "filt", None, None, None),
        P(None, "filt", "slab", None, None),
    )
    out_specs = (
        P(None, "filt", "slab", None, None),
        P(None, "filt", None, None, None),
        P(None, "filt", None, None, None),
    )
    return jax.shard_map(
        on_device, mesh=mesh, in_specs=in_specs, out_specs=out_specs, check_vma=False
    )
```

```python
import functools

import jax
import jax.numpy as jnp
from jax import lax
from jax.experimental import pallas as pl
from jax.experimental.pallas import tpu as pltpu
from jax.sharding import PartitionSpec as P

BF = jnp.bfloat16
F32 = jnp.float32
MESH = pl.DeviceIdType.MESH
VMEM = pl.BlockSpec(memory_space=pltpu.VMEM)
TAPS = 27
W1_BLOCKS = 4


def silu_value(values):
    return values * jax.nn.sigmoid(values)


def silu_slope(values):
    logistic = jax.nn.sigmoid(values)
    return logistic * (1.0 + values * (1.0 - logistic))


def one_hot(source_of_row, size):
    row = lax.broadcasted_iota(jnp.int32, (size, size), 0)
    column = lax.broadcasted_iota(jnp.int32, (size, size), 1)
    return jnp.where(source_of_row(row) == column, 1.0, 0.0).astype(BF)


def piece_matrices():
    def source(o):
        b, d, h = o >> 7, (o >> 6) & 1, (o >> 4) & 3
        c, i, j = (o >> 2) & 3, (o >> 1) & 1, o & 1
        return (b << 7) + (c << 5) + ((2 * d + i) << 3) + 2 * h + j

    row = lax.broadcasted_iota(jnp.int32, (256, 256), 0)
    column = lax.broadcasted_iota(jnp.int32, (256, 256), 1)
    columns = jnp.where(row == 2 * (column & 127) + (column >> 7), 1.0, 0.0).astype(BF)
    return one_hot(source, 256), columns


def shifted(values, by):
    if by == 0:
        return values
    flat = values.reshape(-1, 128)
    lane = lax.broadcasted_iota(jnp.int32, flat.shape, 1)
    rolled = pltpu.roll(flat, (-by) % 128, 1)
    return jnp.where(lane == (127 if by > 0 else 0), 0.0, rolled).reshape(values.shape)


def tap(a, e, g):
    return ((a * 3 + e) * 3 + g) * 8


def nt_dot(a, b):
    return lax.dot_general(a, b, (((1,), (1,)), ((), ())), preferred_element_type=F32)


def remote(source, target, send, recv, axis, to):
    return pltpu.make_async_remote_copy(
        src_ref=source,
        dst_ref=target,
        send_sem=send,
        recv_sem=recv,
        device_id={axis: to},
        device_id_type=MESH,
    )


def repeat(low, high, step):
    lax.fori_loop(low, high, lambda i, carry: (step(i), carry)[1], 0)


class Ring:
    def __init__(self, f, buffer, send, recv):
        self.column, self.y = lax.div(f, 8), lax.rem(f, 8)
        self.buffer, self.send, self.recv = buffer, send, recv

    def device(self, c, y):
        return lax.rem(self.column + c, 2) * 8 + lax.rem(y + 8, 8)

    def piece(self, c, way, h):
        return self.device(c, self.y - h if way == 0 else self.y + h)

    def hop(self, c, way, h):
        block = self.buffer.at[self.piece(c, way, h - 1)]
        to = self.device(0, self.y + 1 if way == 0 else self.y - 1)
        at = c * 2 + way
        return remote(
            block, block, self.send.at[at, h], self.recv.at[at, h], "filt", to
        )

    def cross(self):
        block = self.buffer.at[self.device(0, self.y)]
        return remote(
            block, block, self.send.at[0, 0], self.recv.at[0, 0],
            "filt", self.device(1, self.y),
        )

    def landed(self, c, way, h):
        block = self.buffer.at[self.piece(c, way, h)]
        at = c * 2 + way
        remote(
            block, block, self.send.at[at, h], self.recv.at[at, h],
            "filt", self.device(0, self.y),
        ).wait_recv()

    def run(self, use):
        self.cross().start()
        self.hop(0, 0, 1).start()
        self.hop(0, 1, 1).start()
        use(self.piece(0, 0, 0))
        partner = self.buffer.at[self.device(1, self.y)]
        remote(
            partner, partner, self.send.at[0, 0], self.recv.at[0, 0],
            "filt", self.device(1, self.y),
        ).wait_recv()
        self.hop(1, 0, 1).start()
        self.hop(1, 1, 1).start()
        use(self.piece(1, 0, 0))

        def step(h):
            for c in range(2):
                self.landed(c, 0, h)
                self.hop(c, 0, h + 1).start()
                self.landed(c, 1, h)

                @pl.when(h < 3)
                def _():
                    self.hop(c, 1, h + 1).start()

                use(self.piece(c, 0, h))
                use(self.piece(c, 1, h))

        repeat(1, 4, step)
        for c in range(2):
            self.landed(c, 0, 4)
            use(self.piece(c, 0, 4))

    def sent(self):
        self.cross().wait_send()

        def step(h):
            for c in range(2):
                self.hop(c, 0, h).wait_send()
                self.hop(c, 1, h).wait_send()

        repeat(1, 4, step)
        for c in range(2):
            self.hop(c, 0, 4).wait_send()


class Scatter:
    def __init__(self, n, me, first, count, blocks, landing, total, out, sems):
        self.n, self.me, self.first = n, me, first
        self.owners, self.per = count
        self.blocks, self.landing, self.total, self.out = blocks, landing, total, out
        self.send_a, self.recv_a, self.send_b, self.recv_b = sems

    def owner(self, j):
        return lax.rem(self.first + j, self.n)

    def index(self):
        return lax.rem(self.me - self.first + self.n, self.n)

    def out_copy(self, j):
        return remote(
            self.blocks.at[pl.ds(j * self.per, self.per)],
            self.landing.at[self.me],
            self.send_a.at[j],
            self.recv_a.at[self.me],
            "slab",
            self.owner(j),
        )

    def in_copy(self, source):
        return remote(
            self.total,
            self.landing.at[source],
            self.send_a.at[0],
            self.recv_a.at[source],
            "slab",
            source,
        )

    def back_copy(self, r):
        at = self.index() * self.per
        return remote(
            self.total,
            self.out.at[pl.ds(at, self.per)],
            self.send_b.at[r],
            self.recv_b.at[self.index()],
            "slab",
            lax.rem(self.me + r, self.n),
        )

    def each_owner(self, step):
        def one(j):
            @pl.when(self.owner(j) != self.me)
            def _():
                step(j)

        repeat(0, self.owners, one)

    def start(self):
        self.each_owner(lambda j: self.out_copy(j).start())

    def reduce(self):
        @pl.when(self.index() < self.owners)
        def _():
            at = pl.ds(self.index() * self.per, self.per)

            def add(r, total):
                source = lax.rem(self.me + self.n - r, self.n)
                self.in_copy(source).wait_recv()
                return total + self.landing[source]

            total = lax.fori_loop(1, self.n, add, self.blocks[at])
            self.total[...] = total
            self.out[at] = total
            repeat(1, self.n, lambda r: self.back_copy(r).start())

    def finish(self):
        def arrive(j):
            remote(
                self.total,
                self.out.at[pl.ds(j * self.per, self.per)],
                self.send_b.at[0],
                self.recv_b.at[j],
                "slab",
                self.owner(j),
            ).wait_recv()

        self.each_owner(arrive)
        self.each_owner(lambda j: self.out_copy(j).wait_send())

        @pl.when(self.index() < self.owners)
        def _():
            repeat(1, self.n, lambda r: self.back_copy(r).wait_send())


def level_kernel(
    filts, slabs, two_count, one_count,
    x_ref, w1_ref, w2_ref, og_ref,
    result_ref, two_out, one_out,
    piece, x_all, w_all, hid, y, own, up, down, below, above,
    sg, sg_below, sg_above, view, s, mid, mid_in, dw1, dw1_in, w2_t, pre_ref,
    two, two_in, two_sum, one, one_in, one_sum,
    og, res, fs, fr, gs, gr, hs, hr, ts_a, tr_a, ts_b, tr_b, os_a, or_a, os_b, or_b,
):
    f, z = lax.axis_index("filt"), lax.axis_index("slab")
    barrier = pltpu.get_barrier_semaphore()

    def greet(axis, me, n):
        def one_peer(r):
            pl.semaphore_signal(
                barrier,
                inc=1,
                device_id={axis: lax.rem(me + r, n)},
                device_id_type=MESH,
            )

        repeat(1, n, one_peer)

    greet("filt", f, filts)
    greet("slab", z, slabs)

    def peer(r):
        return lax.rem(f + r, filts)

    def source(r):
        return lax.rem(f + filts - r, filts)

    def filt(i, r, block, target):
        return remote(block, target, fs.at[i, r], fr.at[i, r], "filt", peer(r))

    def to_all(step):
        repeat(1, filts, step)

    rows, columns = piece_matrices()
    half = jnp.dot(rows, x_ref[...], preferred_element_type=F32).astype(BF)
    cut = jnp.dot(half, columns, preferred_element_type=F32).astype(BF)
    piece[...] = cut.reshape(piece.shape)
    x_all[f] = piece[f]
    w_all[f] = w1_ref[...]
    pl.semaphore_wait(barrier, filts + slabs - 2)

    def send_x(r):
        filt(0, r, piece.at[peer(r)], x_all.at[f]).start()
        filt(1, r, w1_ref, w_all.at[f]).start()

    to_all(send_x)
    for b in range(2):
        for d in range(2):
            for n in range(8):
                og[d, b, :, n, :] = og_ref[b, n, d].astype(F32)
    eye = one_hot(lambda o: o, 128)
    w2_t[...] = nt_dot(eye, w2_ref[...]).astype(BF)
    y[:, :, 0] = jnp.zeros((2, 2, 216, 128), F32)
    y[:, :, 5] = jnp.zeros((2, 2, 216, 128), F32)
    view[:, :, :, 0] = jnp.zeros((3, 2, 4, 8, 128), F32)
    view[:, :, :, 5] = jnp.zeros((3, 2, 4, 8, 128), F32)

    def get_x(r):
        filt(0, r, piece.at[peer(r)], x_all.at[source(r)]).wait_recv()
        filt(1, r, w1_ref, w_all.at[source(r)]).wait_recv()

    to_all(get_x)
    x = x_all[...].reshape(256, 256)
    w = w_all[...].reshape(128, 512)
    pre = jnp.dot(w[:, :256], x[:, :128], preferred_element_type=F32)
    pre += jnp.dot(w[:, 256:], x[:, 128:], preferred_element_type=F32)
    pre_ref[...] = pre
    hid[f] = silu_value(pre).astype(BF)

    def spread(q):
        b, d, h = lax.div(q, 8), lax.rem(lax.div(q, 4), 2), lax.rem(q, 4)
        y[b, d, h + 1] = jnp.dot(w2_ref[...], hid[q], preferred_element_type=F32)

    ring = Ring(f, hid, gs, gr)
    ring.run(spread)
    for d in (-1, 2, 0, 1):
        total = None
        for g in range(3):
            part = None
            for a in range(3):
                plane = d + a - 1
                if plane < 0 or plane > 1:
                    continue
                for e in range(3):
                    at = tap(a, e, g)
                    term = y[:, plane, e : e + 4, at : at + 8, :]
                    part = term if part is None else part + term
            part = shifted(part, g - 1)
            total = part if total is None else total + part
        if d < 0:
            down[...] = total
        elif d > 1:
            up[...] = total
        else:
            own[d] = total

    after, before = lax.rem(z + 1, slabs), lax.rem(z + slabs - 1, slabs)

    def rims(i, block_up, block_down, from_below, from_above):
        return (
            remote(block_up, from_below, hs.at[i], hr.at[i], "slab", after),
            remote(block_down, from_above, hs.at[i + 1], hr.at[i + 1], "slab", before),
        )

    first_rims = rims(0, up, down, below, above)
    for copy in first_rims:
        copy.start()
    inside = (z > 0, z < slabs - 1)
    for copy in first_rims:
        copy.wait_recv()
    for d in range(2):
        rim = (below if d == 0 else above)[...]
        second_pre = own[d] + jnp.where(inside[d], rim, 0.0)
        res[d] = silu_value(second_pre)
        grad = og[d] * silu_slope(second_pre)
        sg[d] = grad.astype(BF)
    second_rims = rims(2, sg.at[1], sg.at[0], sg_below, sg_above)
    for copy in second_rims:
        copy.start()

    def put_view(plane, values):
        for g in range(3):
            view[g, :, plane + 1, 1:5] = shifted(values, 1 - g)

    for d in range(2):
        put_view(d, sg[d].astype(F32))
        for b in range(2):
            for n in range(8):
                result_ref[b, n, d] = res[d, b, :, n, :].astype(BF)
    for copy in second_rims:
        copy.wait_recv()
    put_view(-1, jnp.where(inside[0], sg_below[...].astype(F32), 0.0))
    put_view(2, jnp.where(inside[1], sg_above[...].astype(F32), 0.0))
    for d in range(2):
        for a in range(3):
            for e in range(3):
                for g in range(3):
                    at = tap(a, e, g)
                    s[:, d, :, at : at + 8, :] = view[g, :, d - a + 2, 2 - e : 6 - e]

    def back(q, total):
        b, d, h = lax.div(q, 8), lax.rem(lax.div(q, 4), 2), lax.rem(q, 4)
        taps = s[b, d, h].astype(BF)
        mid[q] = jnp.dot(w2_t[...], taps, preferred_element_type=F32).astype(BF)
        return total + nt_dot(taps, hid[q])

    total = lax.fori_loop(0, 16, back, jnp.zeros((216, 128), F32))
    to_all(lambda r: filt(3, r, mid.at[peer(r)], mid_in.at[f]).start())
    two[:TAPS] = total.reshape(TAPS, 8, 128)
    two_sums = Scatter(
        slabs, z, 0, two_count, two, two_in, two_sum, two_out, (ts_a, tr_a, ts_b, tr_b)
    )
    two_sums.start()

    def get_mid(r, total):
        filt(3, r, mid.at[peer(r)], mid_in.at[source(r)]).wait_recv()
        return total + mid_in[source(r)].astype(F32)

    mid_grad = lax.fori_loop(1, filts, get_mid, mid[f].astype(F32))
    grad = (mid_grad * silu_slope(pre_ref[...])).astype(BF)
    x = x_all[...].reshape(256, 256)
    for k in range(2):
        part = nt_dot(grad, x[:, k * 128 : (k + 1) * 128])
        dw1[:, :, k * 256 : (k + 1) * 256] = part.reshape(16, 8, 256)
    to_all(lambda r: filt(4, r, dw1.at[peer(r)], dw1_in.at[f]).start())
    two_sums.reduce()

    def get_one(r, total):
        filt(4, r, dw1.at[peer(r)], dw1_in.at[source(r)]).wait_recv()
        return total + dw1_in[source(r)]

    first = lax.fori_loop(1, filts, get_one, dw1[f])
    for j in range(W1_BLOCKS):
        one[j] = first[:, j * 128 : (j + 1) * 128]
    one_first = TAPS if slabs >= TAPS + W1_BLOCKS else 0
    one_sums = Scatter(
        slabs, z, one_first, one_count, one, one_in, one_sum, one_out,
        (os_a, or_a, os_b, or_b),
    )
    one_sums.start()
    one_sums.reduce()
    two_sums.finish()
    one_sums.finish()

    def sent(r):
        filt(0, r, piece.at[peer(r)], x_all.at[f]).wait_send()
        filt(1, r, w1_ref, w_all.at[f]).wait_send()
        filt(3, r, mid.at[peer(r)], mid_in.at[f]).wait_send()
        filt(4, r, dw1.at[peer(r)], dw1_in.at[f]).wait_send()

    to_all(sent)
    ring.sent()
    for copy in first_rims + second_rims:
        copy.wait_send()


def owners(blocks, n):
    per = -(-blocks // n)
    return -(-blocks // per), per


def level(x, w1, w2, og):
    filts, slabs = lax.axis_size("filt"), lax.axis_size("slab")
    two_count, one_count = owners(TAPS, slabs), owners(W1_BLOCKS, slabs)
    two_size, one_size = (c[0] * c[1] for c in (two_count, one_count))
    sem = pltpu.SemaphoreType.DMA
    buffers = [
        ((16, 16, 256), BF), ((16, 16, 256), BF), ((16, 8, 512), BF),
        ((16, 128, 128), BF), ((2, 2, 6, 216, 128), F32), ((2, 2, 4, 8, 128), F32),
        ((2, 4, 8, 128), F32), ((2, 4, 8, 128), F32),
        ((2, 4, 8, 128), F32), ((2, 4, 8, 128), F32),
        ((2, 2, 4, 8, 128), BF), ((2, 4, 8, 128), BF), ((2, 4, 8, 128), BF),
        ((3, 2, 4, 6, 8, 128), F32), ((2, 2, 4, 216, 128), F32),
        ((16, 128, 128), BF), ((16, 128, 128), BF),
        ((16, 8, 512), F32), ((16, 8, 512), F32), ((128, 216), BF), ((128, 128), F32),
        ((two_size, 8, 128), F32), ((slabs, two_count[1], 8, 128), F32),
        ((two_count[1], 8, 128), F32),
        ((one_size, 8, 128), F32), ((slabs, one_count[1], 8, 128), F32),
        ((one_count[1], 8, 128), F32),
        ((2, 2, 4, 8, 128), F32), ((2, 2, 4, 8, 128), F32),
    ]
    return pl.pallas_call(
        functools.partial(level_kernel, filts, slabs, two_count, one_count),
        out_shape=[
            jax.ShapeDtypeStruct((2, 8, 2, 4, 128), BF),
            jax.ShapeDtypeStruct((two_size, 8, 128), F32),
            jax.ShapeDtypeStruct((one_size, 8, 128), F32),
        ],
        in_specs=[VMEM] * 4,
        out_specs=[VMEM] * 3,
        scratch_shapes=[pltpu.VMEM(shape, dtype) for shape, dtype in buffers]
        + [
            sem((5, filts)), sem((5, filts)), sem((4, 5)), sem((4, 5)), sem((4,)), sem((4,)),
            sem((two_count[0],)), sem((slabs,)), sem((slabs,)), sem((two_count[0],)),
            sem((one_count[0],)), sem((slabs,)), sem((slabs,)), sem((one_count[0],)),
        ],
        compiler_params=pltpu.CompilerParams(collective_id=1, has_side_effects=True),
        name="level",
    )(x, w1, w2, og)


def on_device(volume, first_weight, second_weight, out_grad):
    w1 = first_weight.transpose(1, 4, 0, 2, 3).reshape(8, 512)
    w2 = second_weight.transpose(2, 3, 4, 1, 0).reshape(216, 128)
    result, two, one = level(volume.reshape(256, 256), w1, w2, out_grad)
    weight_two = two[:TAPS].reshape(3, 3, 3, 8, 128).transpose(4, 3, 0, 1, 2)
    one = one.reshape(2, 2, 8, 32, 2, 2).transpose(1, 3, 2, 4, 5, 0)
    weight_one = one.reshape(64, 8, 2, 2, 2)
    return (result, weight_one, weight_two)


def solution(mesh):
    in_specs = (
        P(None, "filt", "slab", None, None),
        P(None, "filt", None, None, None),
        P(None, "filt", None, None, None),
        P(None, "filt", "slab", None, None),
    )
    out_specs = (
        P(None, "filt", "slab", None, None),
        P(None, "filt", None, None, None),
        P(None, "filt", None, None, None),
    )
    return jax.shard_map(
        on_device, mesh=mesh, in_specs=in_specs, out_specs=out_specs, check_vma=False
    )
```

```python
import functools

import jax
import jax.numpy as jnp
from jax import lax
from jax.experimental import pallas as pl
from jax.experimental.pallas import tpu as pltpu
from jax.sharding import PartitionSpec as P

BF = jnp.bfloat16
F32 = jnp.float32
MESH = pl.DeviceIdType.MESH
VMEM = pl.BlockSpec(memory_space=pltpu.VMEM)
TAPS = 27
W1_BLOCKS = 4


def silu_value(values):
    return values * jax.nn.sigmoid(values)


def silu_slope(values):
    logistic = jax.nn.sigmoid(values)
    return logistic * (1.0 + values * (1.0 - logistic))


def one_hot(source_of_row, size):
    row = lax.broadcasted_iota(jnp.int32, (size, size), 0)
    column = lax.broadcasted_iota(jnp.int32, (size, size), 1)
    return jnp.where(source_of_row(row) == column, 1.0, 0.0).astype(BF)


def piece_matrices():
    def source(o):
        b, d, h = o >> 7, (o >> 6) & 1, (o >> 4) & 3
        c, i, j = (o >> 2) & 3, (o >> 1) & 1, o & 1
        return (b << 7) + (c << 5) + ((2 * d + i) << 3) + 2 * h + j

    row = lax.broadcasted_iota(jnp.int32, (256, 256), 0)
    column = lax.broadcasted_iota(jnp.int32, (256, 256), 1)
    columns = jnp.where(row == 2 * (column & 127) + (column >> 7), 1.0, 0.0).astype(BF)
    return one_hot(source, 256), columns


def shifted(values, by):
    if by == 0:
        return values
    flat = values.reshape(-1, 128)
    lane = lax.broadcasted_iota(jnp.int32, flat.shape, 1)
    rolled = pltpu.roll(flat, (-by) % 128, 1)
    return jnp.where(lane == (127 if by > 0 else 0), 0.0, rolled).reshape(values.shape)


def tap(a, e, g):
    return ((a * 3 + e) * 3 + g) * 8


def nt_dot(a, b):
    return lax.dot_general(a, b, (((1,), (1,)), ((), ())), preferred_element_type=F32)


def remote(source, target, send, recv, axis, to):
    return pltpu.make_async_remote_copy(
        src_ref=source,
        dst_ref=target,
        send_sem=send,
        recv_sem=recv,
        device_id={axis: to},
        device_id_type=MESH,
    )


def repeat(low, high, step):
    lax.fori_loop(low, high, lambda i, carry: (step(i), carry)[1], 0)


class Scatter:
    def __init__(self, n, me, first, count, blocks, landing, total, out, sems):
        self.n, self.me, self.first = n, me, first
        self.owners, self.per = count
        self.blocks, self.landing, self.total, self.out = blocks, landing, total, out
        self.send_a, self.recv_a, self.send_b, self.recv_b = sems

    def owner(self, j):
        return lax.rem(self.first + j, self.n)

    def index(self):
        return lax.rem(self.me - self.first + self.n, self.n)

    def out_copy(self, j):
        return remote(
            self.blocks.at[pl.ds(j * self.per, self.per)],
            self.landing.at[self.me],
            self.send_a.at[j],
            self.recv_a.at[self.me],
            "slab",
            self.owner(j),
        )

    def in_copy(self, source):
        return remote(
            self.total,
            self.landing.at[source],
            self.send_a.at[0],
            self.recv_a.at[source],
            "slab",
            source,
        )

    def back_copy(self, r):
        at = self.index() * self.per
        return remote(
            self.total,
            self.out.at[pl.ds(at, self.per)],
            self.send_b.at[r],
            self.recv_b.at[self.index()],
            "slab",
            lax.rem(self.me + r, self.n),
        )

    def each_owner(self, step):
        def one(j):
            @pl.when(self.owner(j) != self.me)
            def _():
                step(j)

        repeat(0, self.owners, one)

    def start(self):
        self.each_owner(lambda j: self.out_copy(j).start())

    def reduce(self):
        @pl.when(self.index() < self.owners)
        def _():
            at = pl.ds(self.index() * self.per, self.per)

            def add(r, total):
                source = lax.rem(self.me + self.n - r, self.n)
                self.in_copy(source).wait_recv()
                return total + self.landing[source]

            total = lax.fori_loop(1, self.n, add, self.blocks[at])
            self.total[...] = total
            self.out[at] = total
            repeat(1, self.n, lambda r: self.back_copy(r).start())

    def finish(self):
        def arrive(j):
            remote(
                self.total,
                self.out.at[pl.ds(j * self.per, self.per)],
                self.send_b.at[0],
                self.recv_b.at[j],
                "slab",
                self.owner(j),
            ).wait_recv()

        self.each_owner(arrive)
        self.each_owner(lambda j: self.out_copy(j).wait_send())

        @pl.when(self.index() < self.owners)
        def _():
            repeat(1, self.n, lambda r: self.back_copy(r).wait_send())


def level_kernel(
    filts, slabs, two_count, one_count,
    x_ref, w1_ref, w2_ref, og_ref,
    result_ref, two_out, one_out,
    piece, x_all, w_all, hid, y, own, up, down, below, above,
    sg, sg_below, sg_above, view, s, mid, mid_in, dw1, dw1_in, w2_t, pre_ref,
    two, two_in, two_sum, one, one_in, one_sum,
    og, res, fs, fr, hs, hr, ts_a, tr_a, ts_b, tr_b, os_a, or_a, os_b, or_b,
):
    f, z = lax.axis_index("filt"), lax.axis_index("slab")
    barrier = pltpu.get_barrier_semaphore()

    def greet(axis, me, n):
        def one_peer(r):
            pl.semaphore_signal(
                barrier,
                inc=1,
                device_id={axis: lax.rem(me + r, n)},
                device_id_type=MESH,
            )

        repeat(1, n, one_peer)

    greet("filt", f, filts)
    greet("slab", z, slabs)

    def other(r, sign):
        m = lax.div(r, 2)
        dy = 4 + (1 - 2 * lax.rem(m, 2)) * lax.div(m + 1, 2)
        column = lax.rem(lax.div(f, 8) + 1 + lax.rem(r, 2), 2)
        return column * 8 + lax.rem(lax.rem(f, 8) + 8 + sign * dy, 8)

    def peer(r):
        return other(r, 1)

    def source(r):
        return other(r, -1)

    def filt(i, r, block, target):
        return remote(block, target, fs.at[i, r], fr.at[i, r], "filt", peer(r))

    def to_all(step):
        repeat(0, filts - 1, step)

    def from_all(step, start):
        return lax.fori_loop(
            0, filts - 1, lambda r, carry: step(filts - 2 - r, carry), start
        )

    rows, columns = piece_matrices()
    half = jnp.dot(rows, x_ref[...], preferred_element_type=F32).astype(BF)
    cut = jnp.dot(half, columns, preferred_element_type=F32).astype(BF)
    piece[...] = cut.reshape(piece.shape)
    x_all[f] = piece[f]
    w_all[f] = w1_ref[...]
    pl.semaphore_wait(barrier, filts + slabs - 2)

    def send_x(r):
        filt(0, r, piece.at[peer(r)], x_all.at[f]).start()
        filt(1, r, w1_ref, w_all.at[f]).start()

    to_all(send_x)
    for b in range(2):
        for d in range(2):
            for n in range(8):
                og[d, b, :, n, :] = og_ref[b, n, d].astype(F32)
    eye = one_hot(lambda o: o, 128)
    w2_t[...] = nt_dot(eye, w2_ref[...]).astype(BF)
    y[:, :, 0] = jnp.zeros((2, 2, 216, 128), F32)
    y[:, :, 5] = jnp.zeros((2, 2, 216, 128), F32)
    view[:, :, :, 0] = jnp.zeros((3, 2, 4, 8, 128), F32)
    view[:, :, :, 5] = jnp.zeros((3, 2, 4, 8, 128), F32)

    def get_x(r):
        filt(0, r, piece.at[peer(r)], x_all.at[source(r)]).wait_recv()
        filt(1, r, w1_ref, w_all.at[source(r)]).wait_recv()

    to_all(get_x)
    x = x_all[...].reshape(256, 256)
    w = w_all[...].reshape(128, 512)
    pre = jnp.dot(w[:, :256], x[:, :128], preferred_element_type=F32)
    pre += jnp.dot(w[:, 256:], x[:, 128:], preferred_element_type=F32)
    pre_ref[...] = pre
    hid[f] = silu_value(pre).astype(BF)
    to_all(lambda r: filt(2, r, hid.at[f], hid.at[f]).start())

    def spread(q):
        b, d, h = lax.div(q, 8), lax.rem(lax.div(q, 4), 2), lax.rem(q, 4)
        y[b, d, h + 1] = jnp.dot(w2_ref[...], hid[q], preferred_element_type=F32)

    spread(f)

    def get_hidden(r):
        filt(2, r, hid.at[f], hid.at[source(r)]).wait_recv()
        spread(source(r))

    from_all(lambda r, carry: (get_hidden(r), carry)[1], 0)
    for d in (-1, 2, 0, 1):
        total = None
        for g in range(3):
            part = None
            for a in range(3):
                plane = d + a - 1
                if plane < 0 or plane > 1:
                    continue
                for e in range(3):
                    at = tap(a, e, g)
                    term = y[:, plane, e : e + 4, at : at + 8, :]
                    part = term if part is None else part + term
            part = shifted(part, g - 1)
            total = part if total is None else total + part
        if d < 0:
            down[...] = total
        elif d > 1:
            up[...] = total
        else:
            own[d] = total

    after, before = lax.rem(z + 1, slabs), lax.rem(z + slabs - 1, slabs)

    def rims(i, block_up, block_down, from_below, from_above):
        return (
            remote(block_up, from_below, hs.at[i], hr.at[i], "slab", after),
            remote(block_down, from_above, hs.at[i + 1], hr.at[i + 1], "slab", before),
        )

    first_rims = rims(0, up, down, below, above)
    for copy in first_rims:
        copy.start()
    inside = (z > 0, z < slabs - 1)
    for copy in first_rims:
        copy.wait_recv()
    for d in range(2):
        rim = (below if d == 0 else above)[...]
        second_pre = own[d] + jnp.where(inside[d], rim, 0.0)
        res[d] = silu_value(second_pre)
        grad = og[d] * silu_slope(second_pre)
        sg[d] = grad.astype(BF)
    second_rims = rims(2, sg.at[1], sg.at[0], sg_below, sg_above)
    for copy in second_rims:
        copy.start()

    def put_view(plane, values):
        for g in range(3):
            view[g, :, plane + 1, 1:5] = shifted(values, 1 - g)

    for d in range(2):
        put_view(d, sg[d].astype(F32))
        for b in range(2):
            for n in range(8):
                result_ref[b, n, d] = res[d, b, :, n, :].astype(BF)

    def put_taps(d, a):
        for e in range(3):
            for g in range(3):
                at = tap(a, e, g)
                s[:, d, :, at : at + 8, :] = view[g, :, d - a + 2, 2 - e : 6 - e]

    for d in range(2):
        put_taps(d, 1)
        put_taps(d, 2 * d)
    for copy in second_rims:
        copy.wait_recv()
    put_view(-1, jnp.where(inside[0], sg_below[...].astype(F32), 0.0))
    put_view(2, jnp.where(inside[1], sg_above[...].astype(F32), 0.0))
    for d in range(2):
        put_taps(d, 2 - 2 * d)

    def taps_of(q):
        b, d, h = lax.div(q, 8), lax.rem(lax.div(q, 4), 2), lax.rem(q, 4)
        return s[b, d, h].astype(BF)

    def back(q):
        part = jnp.dot(w2_t[...], taps_of(q), preferred_element_type=F32)
        mid[q] = part.astype(BF)

    def send_mid(r):
        filt(3, r, mid.at[peer(r)], mid_in.at[f]).start()

    back(peer(0))

    def back_step(r):
        back(peer(r))
        send_mid(r - 1)

    repeat(1, filts - 1, back_step)
    back(f)
    send_mid(filts - 2)
    total = lax.fori_loop(
        0,
        filts,
        lambda q, total: total + nt_dot(taps_of(q), hid[q]),
        jnp.zeros((216, 128), F32),
    )
    two[:TAPS] = total.reshape(TAPS, 8, 128)
    two_sums = Scatter(
        slabs, z, 0, two_count, two, two_in, two_sum, two_out, (ts_a, tr_a, ts_b, tr_b)
    )
    two_sums.start()

    def get_mid(r, total):
        filt(3, r, mid.at[peer(r)], mid_in.at[source(r)]).wait_recv()
        return total + mid_in[source(r)].astype(F32)

    mid_grad = from_all(get_mid, mid[f].astype(F32))
    grad = (mid_grad * silu_slope(pre_ref[...])).astype(BF)
    x = x_all[...].reshape(256, 256)
    for k in range(2):
        part = nt_dot(grad, x[:, k * 128 : (k + 1) * 128])
        dw1[:, :, k * 256 : (k + 1) * 256] = part.reshape(16, 8, 256)
    to_all(lambda r: filt(4, r, dw1.at[peer(r)], dw1_in.at[f]).start())
    two_sums.reduce()

    def get_one(r, total):
        filt(4, r, dw1.at[peer(r)], dw1_in.at[source(r)]).wait_recv()
        return total + dw1_in[source(r)]

    first = from_all(get_one, dw1[f])
    for j in range(W1_BLOCKS):
        one[j] = first[:, j * 128 : (j + 1) * 128]
    one_first = TAPS if slabs >= TAPS + W1_BLOCKS else 0
    one_sums = Scatter(
        slabs, z, one_first, one_count, one, one_in, one_sum, one_out,
        (os_a, or_a, os_b, or_b),
    )
    one_sums.start()

    def sent(r):
        filt(0, r, piece.at[peer(r)], x_all.at[f]).wait_send()
        filt(1, r, w1_ref, w_all.at[f]).wait_send()
        filt(2, r, hid.at[f], hid.at[f]).wait_send()
        filt(3, r, mid.at[peer(r)], mid_in.at[f]).wait_send()
        filt(4, r, dw1.at[peer(r)], dw1_in.at[f]).wait_send()

    to_all(sent)
    for copy in first_rims + second_rims:
        copy.wait_send()
    one_sums.reduce()
    two_sums.finish()
    one_sums.finish()


def owners(blocks, n):
    per = -(-blocks // n)
    return -(-blocks // per), per


def level(x, w1, w2, og):
    filts, slabs = lax.axis_size("filt"), lax.axis_size("slab")
    two_count, one_count = owners(TAPS, slabs), owners(W1_BLOCKS, slabs)
    two_size, one_size = (c[0] * c[1] for c in (two_count, one_count))
    sem = pltpu.SemaphoreType.DMA
    buffers = [
        ((16, 16, 256), BF), ((16, 16, 256), BF), ((16, 8, 512), BF),
        ((16, 128, 128), BF), ((2, 2, 6, 216, 128), F32), ((2, 2, 4, 8, 128), F32),
        ((2, 4, 8, 128), F32), ((2, 4, 8, 128), F32),
        ((2, 4, 8, 128), F32), ((2, 4, 8, 128), F32),
        ((2, 2, 4, 8, 128), BF), ((2, 4, 8, 128), BF), ((2, 4, 8, 128), BF),
        ((3, 2, 4, 6, 8, 128), F32), ((2, 2, 4, 216, 128), F32),
        ((16, 128, 128), BF), ((16, 128, 128), BF),
        ((16, 8, 512), F32), ((16, 8, 512), F32), ((128, 216), BF), ((128, 128), F32),
        ((two_size, 8, 128), F32), ((slabs, two_count[1], 8, 128), F32),
        ((two_count[1], 8, 128), F32),
        ((one_size, 8, 128), F32), ((slabs, one_count[1], 8, 128), F32),
        ((one_count[1], 8, 128), F32),
        ((2, 2, 4, 8, 128), F32), ((2, 2, 4, 8, 128), F32),
    ]
    return pl.pallas_call(
        functools.partial(level_kernel, filts, slabs, two_count, one_count),
        out_shape=[
            jax.ShapeDtypeStruct((2, 8, 2, 4, 128), BF),
            jax.ShapeDtypeStruct((two_size, 8, 128), F32),
            jax.ShapeDtypeStruct((one_size, 8, 128), F32),
        ],
        in_specs=[VMEM] * 4,
        out_specs=[VMEM] * 3,
        scratch_shapes=[pltpu.VMEM(shape, dtype) for shape, dtype in buffers]
        + [
            sem((5, filts)), sem((5, filts)), sem((4,)), sem((4,)),
            sem((two_count[0],)), sem((slabs,)), sem((slabs,)), sem((two_count[0],)),
            sem((one_count[0],)), sem((slabs,)), sem((slabs,)), sem((one_count[0],)),
        ],
        compiler_params=pltpu.CompilerParams(collective_id=1, has_side_effects=True),
        name="level",
    )(x, w1, w2, og)


def on_device(volume, first_weight, second_weight, out_grad):
    w1 = first_weight.transpose(1, 4, 0, 2, 3).reshape(8, 512)
    w2 = second_weight.transpose(2, 3, 4, 1, 0).reshape(216, 128)
    result, two, one = level(volume.reshape(256, 256), w1, w2, out_grad)
    weight_two = two[:TAPS].reshape(3, 3, 3, 8, 128).transpose(4, 3, 0, 1, 2)
    one = one.reshape(2, 2, 8, 32, 2, 2).transpose(1, 3, 2, 4, 5, 0)
    weight_one = one.reshape(64, 8, 2, 2, 2)
    return (result, weight_one, weight_two)


def solution(mesh):
    in_specs = (
        P(None, "filt", "slab", None, None),
        P(None, "filt", None, None, None),
        P(None, "filt", None, None, None),
        P(None, "filt", "slab", None, None),
    )
    out_specs = (
        P(None, "filt", "slab", None, None),
        P(None, "filt", None, None, None),
        P(None, "filt", None, None, None),
    )
    return jax.shard_map(
        on_device, mesh=mesh, in_specs=in_specs, out_specs=out_specs, check_vma=False
    )
```

```python
import functools

import jax
import jax.numpy as jnp
from jax import lax
from jax.experimental import pallas as pl
from jax.experimental.pallas import tpu as pltpu
from jax.sharding import PartitionSpec as P

BF = jnp.bfloat16
F32 = jnp.float32
MESH = pl.DeviceIdType.MESH
VMEM = pl.BlockSpec(memory_space=pltpu.VMEM)
ANY = pl.BlockSpec(memory_space=pl.ANY)
TAPS = 27
W1_BLOCKS = 4


def silu_value(values):
    return values * jax.nn.sigmoid(values)


def silu_slope(values):
    logistic = jax.nn.sigmoid(values)
    return logistic * (1.0 + values * (1.0 - logistic))


def one_hot(source_of_row, size):
    row = lax.broadcasted_iota(jnp.int32, (size, size), 0)
    column = lax.broadcasted_iota(jnp.int32, (size, size), 1)
    return jnp.where(source_of_row(row) == column, 1.0, 0.0).astype(BF)


def piece_matrices():
    def source(o):
        b, d, h = o >> 7, (o >> 6) & 1, (o >> 4) & 3
        c, i, j = (o >> 2) & 3, (o >> 1) & 1, o & 1
        return (b << 7) + (c << 5) + ((2 * d + i) << 3) + 2 * h + j

    row = lax.broadcasted_iota(jnp.int32, (256, 256), 0)
    column = lax.broadcasted_iota(jnp.int32, (256, 256), 1)
    columns = jnp.where(row == 2 * (column & 127) + (column >> 7), 1.0, 0.0).astype(BF)
    return one_hot(source, 256), columns


def shifted(values, by):
    if by == 0:
        return values
    flat = values.reshape(-1, 128)
    lane = lax.broadcasted_iota(jnp.int32, flat.shape, 1)
    rolled = pltpu.roll(flat, (-by) % 128, 1)
    return jnp.where(lane == (127 if by > 0 else 0), 0.0, rolled).reshape(values.shape)


def tap(a, e, g):
    return ((a * 3 + e) * 3 + g) * 8


def nt_dot(a, b):
    return lax.dot_general(a, b, (((1,), (1,)), ((), ())), preferred_element_type=F32)


def remote(source, target, send, recv, axis, to):
    return pltpu.make_async_remote_copy(
        src_ref=source,
        dst_ref=target,
        send_sem=send,
        recv_sem=recv,
        device_id={axis: to},
        device_id_type=MESH,
    )


def repeat(low, high, step):
    lax.fori_loop(low, high, lambda i, carry: (step(i), carry)[1], 0)


class Scatter:
    def __init__(self, n, me, first, count, blocks, landing, total, out, sems):
        self.n, self.me, self.first = n, me, first
        self.owners, self.per = count
        self.blocks, self.landing, self.total, self.out = blocks, landing, total, out
        self.send_a, self.recv_a, self.send_b, self.recv_b = sems

    def owner(self, j):
        return lax.rem(self.first + j, self.n)

    def index(self):
        return lax.rem(self.me - self.first + self.n, self.n)

    def out_copy(self, j):
        return remote(
            self.blocks.at[pl.ds(j * self.per, self.per)],
            self.landing.at[self.me],
            self.send_a.at[j],
            self.recv_a.at[self.me],
            "slab",
            self.owner(j),
        )

    def in_copy(self, source):
        return remote(
            self.total,
            self.landing.at[source],
            self.send_a.at[0],
            self.recv_a.at[source],
            "slab",
            source,
        )

    def back_copy(self, r):
        at = self.index() * self.per
        return remote(
            self.total,
            self.out.at[pl.ds(at, self.per)],
            self.send_b.at[r],
            self.recv_b.at[self.index()],
            "slab",
            lax.rem(self.me + r, self.n),
        )

    def each_owner(self, step):
        def one(j):
            @pl.when(self.owner(j) != self.me)
            def _():
                step(j)

        repeat(0, self.owners, one)

    def start(self):
        self.each_owner(lambda j: self.out_copy(j).start())

    def reduce(self):
        @pl.when(self.index() < self.owners)
        def _():
            at = pl.ds(self.index() * self.per, self.per)

            def add(r, total):
                source = lax.rem(self.me + self.n - r, self.n)
                self.in_copy(source).wait_recv()
                return total + self.landing[source]

            total = lax.fori_loop(1, self.n, add, self.blocks[at])
            self.total[...] = total
            self.out[at] = total
            repeat(1, self.n, lambda r: self.back_copy(r).start())

    def finish(self):
        def arrive(j):
            remote(
                self.total,
                self.out.at[pl.ds(j * self.per, self.per)],
                self.send_b.at[0],
                self.recv_b.at[j],
                "slab",
                self.owner(j),
            ).wait_recv()

        self.each_owner(arrive)
        self.each_owner(lambda j: self.out_copy(j).wait_send())

        @pl.when(self.index() < self.owners)
        def _():
            repeat(1, self.n, lambda r: self.back_copy(r).wait_send())


def level_kernel(
    filts, slabs, two_count, one_count,
    x_hbm, w1_ref, w2_hbm, og_hbm,
    result_hbm, two_out, one_out,
    piece, x_all, w_all, hid, y, own, up, down, below, above,
    sg, sg_below, sg_above, view, s, mid, mid_in, dw1, dw1_in, w2_t, pre_ref,
    two, two_in, two_sum, one, one_in, one_sum,
    og, res, x_ref, w2_ref, og_ref, result_ref, ls, fs, fr, hs, hr, ts_a, tr_a, ts_b, tr_b, os_a, or_a, os_b, or_b,
):
    f, z = lax.axis_index("filt"), lax.axis_index("slab")
    barrier = pltpu.get_barrier_semaphore()
    loads = [
        pltpu.make_async_copy(array, place, ls.at[i])
        for i, (array, place) in enumerate(
            ((x_hbm, x_ref), (w2_hbm, w2_ref), (og_hbm, og_ref))
        )
    ]
    for copy in loads:
        copy.start()

    def greet(axis, me, n):
        def one_peer(r):
            pl.semaphore_signal(
                barrier,
                inc=1,
                device_id={axis: lax.rem(me + r, n)},
                device_id_type=MESH,
            )

        repeat(1, n, one_peer)

    greet("filt", f, filts)
    greet("slab", z, slabs)

    def other(r, sign):
        m = lax.div(r, 2)
        dy = 4 + (1 - 2 * lax.rem(m, 2)) * lax.div(m + 1, 2)
        column = lax.rem(lax.div(f, 8) + 1 + lax.rem(r, 2), 2)
        return column * 8 + lax.rem(lax.rem(f, 8) + 8 + sign * dy, 8)

    def peer(r):
        return other(r, 1)

    def source(r):
        return other(r, -1)

    def filt(i, r, block, target):
        return remote(block, target, fs.at[i, r], fr.at[i, r], "filt", peer(r))

    def to_all(step):
        repeat(0, filts - 1, step)

    def from_all(step, start):
        return lax.fori_loop(
            0, filts - 1, lambda r, carry: step(filts - 2 - r, carry), start
        )

    rows, columns = piece_matrices()
    loads[0].wait()
    half = jnp.dot(rows, x_ref[...], preferred_element_type=F32).astype(BF)
    cut = jnp.dot(half, columns, preferred_element_type=F32).astype(BF)
    piece[...] = cut.reshape(piece.shape)
    x_all[f] = piece[f]
    w_all[f] = w1_ref[...]
    pl.semaphore_wait(barrier, filts + slabs - 2)

    def send_x(r):
        filt(0, r, piece.at[peer(r)], x_all.at[f]).start()
        filt(1, r, w1_ref, w_all.at[f]).start()

    to_all(send_x)
    loads[1].wait()
    loads[2].wait()
    for b in range(2):
        for d in range(2):
            for n in range(8):
                og[d, b, :, n, :] = og_ref[b, n, d].astype(F32)
    eye = one_hot(lambda o: o, 128)
    w2_t[...] = nt_dot(eye, w2_ref[...]).astype(BF)
    y[:, :, 0] = jnp.zeros((2, 2, 216, 128), F32)
    y[:, :, 5] = jnp.zeros((2, 2, 216, 128), F32)
    view[:, :, :, 0] = jnp.zeros((3, 2, 4, 8, 128), F32)
    view[:, :, :, 5] = jnp.zeros((3, 2, 4, 8, 128), F32)

    def get_x(r):
        filt(0, r, piece.at[peer(r)], x_all.at[source(r)]).wait_recv()
        filt(1, r, w1_ref, w_all.at[source(r)]).wait_recv()

    to_all(get_x)
    x = x_all[...].reshape(256, 256)
    w = w_all[...].reshape(128, 512)
    pre = jnp.dot(w[:, :256], x[:, :128], preferred_element_type=F32)
    pre += jnp.dot(w[:, 256:], x[:, 128:], preferred_element_type=F32)
    pre_ref[...] = pre
    hid[f] = silu_value(pre).astype(BF)
    to_all(lambda r: filt(2, r, hid.at[f], hid.at[f]).start())

    def spread(q):
        b, d, h = lax.div(q, 8), lax.rem(lax.div(q, 4), 2), lax.rem(q, 4)
        y[b, d, h + 1] = jnp.dot(w2_ref[...], hid[q], preferred_element_type=F32)

    spread(f)

    def get_hidden(r):
        filt(2, r, hid.at[f], hid.at[source(r)]).wait_recv()
        spread(source(r))

    from_all(lambda r, carry: (get_hidden(r), carry)[1], 0)
    for d in (-1, 2, 0, 1):
        total = None
        for g in range(3):
            part = None
            for a in range(3):
                plane = d + a - 1
                if plane < 0 or plane > 1:
                    continue
                for e in range(3):
                    at = tap(a, e, g)
                    term = y[:, plane, e : e + 4, at : at + 8, :]
                    part = term if part is None else part + term
            part = shifted(part, g - 1)
            total = part if total is None else total + part
        if d < 0:
            down[...] = total
        elif d > 1:
            up[...] = total
        else:
            own[d] = total

    after, before = lax.rem(z + 1, slabs), lax.rem(z + slabs - 1, slabs)

    def rims(i, block_up, block_down, from_below, from_above):
        return (
            remote(block_up, from_below, hs.at[i], hr.at[i], "slab", after),
            remote(block_down, from_above, hs.at[i + 1], hr.at[i + 1], "slab", before),
        )

    first_rims = rims(0, up, down, below, above)
    for copy in first_rims:
        copy.start()
    inside = (z > 0, z < slabs - 1)
    for copy in first_rims:
        copy.wait_recv()
    for d in range(2):
        rim = (below if d == 0 else above)[...]
        second_pre = own[d] + jnp.where(inside[d], rim, 0.0)
        res[d] = silu_value(second_pre)
        grad = og[d] * silu_slope(second_pre)
        sg[d] = grad.astype(BF)
    second_rims = rims(2, sg.at[1], sg.at[0], sg_below, sg_above)
    for copy in second_rims:
        copy.start()

    def put_view(plane, values):
        for g in range(3):
            view[g, :, plane + 1, 1:5] = shifted(values, 1 - g)

    for d in range(2):
        put_view(d, sg[d].astype(F32))
        for b in range(2):
            for n in range(8):
                result_ref[b, n, d] = res[d, b, :, n, :].astype(BF)

    def put_taps(d, a):
        for e in range(3):
            for g in range(3):
                at = tap(a, e, g)
                s[:, d, :, at : at + 8, :] = view[g, :, d - a + 2, 2 - e : 6 - e]

    for d in range(2):
        put_taps(d, 1)
        put_taps(d, 2 * d)
    for copy in second_rims:
        copy.wait_recv()
    put_view(-1, jnp.where(inside[0], sg_below[...].astype(F32), 0.0))
    put_view(2, jnp.where(inside[1], sg_above[...].astype(F32), 0.0))
    for d in range(2):
        put_taps(d, 2 - 2 * d)

    def taps_of(q):
        b, d, h = lax.div(q, 8), lax.rem(lax.div(q, 4), 2), lax.rem(q, 4)
        return s[b, d, h].astype(BF)

    def back(q):
        part = jnp.dot(w2_t[...], taps_of(q), preferred_element_type=F32)
        mid[q] = part.astype(BF)

    def send_mid(r):
        filt(3, r, mid.at[peer(r)], mid_in.at[f]).start()

    back(peer(0))

    def back_step(r):
        back(peer(r))
        send_mid(r - 1)

    repeat(1, filts - 1, back_step)
    back(f)
    send_mid(filts - 2)
    total = lax.fori_loop(
        0,
        filts,
        lambda q, total: total + nt_dot(taps_of(q), hid[q]),
        jnp.zeros((216, 128), F32),
    )
    store = pltpu.make_async_copy(result_ref, result_hbm, ls.at[3])
    store.start()
    two[:TAPS] = total.reshape(TAPS, 8, 128)
    two_sums = Scatter(
        slabs, z, 0, two_count, two, two_in, two_sum, two_out, (ts_a, tr_a, ts_b, tr_b)
    )
    two_sums.start()

    def get_mid(r, total):
        filt(3, r, mid.at[peer(r)], mid_in.at[source(r)]).wait_recv()
        return total + mid_in[source(r)].astype(F32)

    mid_grad = from_all(get_mid, mid[f].astype(F32))
    grad = (mid_grad * silu_slope(pre_ref[...])).astype(BF)
    x = x_all[...].reshape(256, 256)
    for k in range(2):
        part = nt_dot(grad, x[:, k * 128 : (k + 1) * 128])
        dw1[:, :, k * 256 : (k + 1) * 256] = part.reshape(16, 8, 256).astype(BF)
    to_all(lambda r: filt(4, r, dw1.at[peer(r)], dw1_in.at[f]).start())
    two_sums.reduce()

    def get_one(r, total):
        filt(4, r, dw1.at[peer(r)], dw1_in.at[source(r)]).wait_recv()
        return total + dw1_in[source(r)].astype(F32)

    first = from_all(get_one, dw1[f].astype(F32))
    for j in range(W1_BLOCKS):
        one[j] = first[:, j * 128 : (j + 1) * 128]
    one_first = TAPS if slabs >= TAPS + W1_BLOCKS else 0
    one_sums = Scatter(
        slabs, z, one_first, one_count, one, one_in, one_sum, one_out,
        (os_a, or_a, os_b, or_b),
    )
    one_sums.start()

    def sent(r):
        filt(0, r, piece.at[peer(r)], x_all.at[f]).wait_send()
        filt(1, r, w1_ref, w_all.at[f]).wait_send()
        filt(2, r, hid.at[f], hid.at[f]).wait_send()
        filt(3, r, mid.at[peer(r)], mid_in.at[f]).wait_send()
        filt(4, r, dw1.at[peer(r)], dw1_in.at[f]).wait_send()

    to_all(sent)
    for copy in first_rims + second_rims:
        copy.wait_send()
    one_sums.reduce()
    two_sums.finish()
    one_sums.finish()
    store.wait()


def owners(blocks, n):
    per = -(-blocks // n)
    return -(-blocks // per), per


def level(x, w1, w2, og):
    filts, slabs = lax.axis_size("filt"), lax.axis_size("slab")
    two_count, one_count = owners(TAPS, slabs), owners(W1_BLOCKS, slabs)
    two_size, one_size = (c[0] * c[1] for c in (two_count, one_count))
    sem = pltpu.SemaphoreType.DMA
    buffers = [
        ((16, 16, 256), BF), ((16, 16, 256), BF), ((16, 8, 512), BF),
        ((16, 128, 128), BF), ((2, 2, 6, 216, 128), F32), ((2, 2, 4, 8, 128), F32),
        ((2, 4, 8, 128), F32), ((2, 4, 8, 128), F32),
        ((2, 4, 8, 128), F32), ((2, 4, 8, 128), F32),
        ((2, 2, 4, 8, 128), BF), ((2, 4, 8, 128), BF), ((2, 4, 8, 128), BF),
        ((3, 2, 4, 6, 8, 128), F32), ((2, 2, 4, 216, 128), F32),
        ((16, 128, 128), BF), ((16, 128, 128), BF),
        ((16, 8, 512), BF), ((16, 8, 512), BF), ((128, 216), BF), ((128, 128), F32),
        ((two_size, 8, 128), F32), ((slabs, two_count[1], 8, 128), F32),
        ((two_count[1], 8, 128), F32),
        ((one_size, 8, 128), F32), ((slabs, one_count[1], 8, 128), F32),
        ((one_count[1], 8, 128), F32),
        ((2, 2, 4, 8, 128), F32), ((2, 2, 4, 8, 128), F32),
        ((256, 256), BF), ((216, 128), BF), ((2, 8, 2, 4, 128), BF),
        ((2, 8, 2, 4, 128), BF),
    ]
    return pl.pallas_call(
        functools.partial(level_kernel, filts, slabs, two_count, one_count),
        out_shape=[
            jax.ShapeDtypeStruct((2, 8, 2, 4, 128), BF),
            jax.ShapeDtypeStruct((two_size, 8, 128), F32),
            jax.ShapeDtypeStruct((one_size, 8, 128), F32),
        ],
        in_specs=[ANY, VMEM, ANY, ANY],
        out_specs=[ANY, VMEM, VMEM],
        scratch_shapes=[pltpu.VMEM(shape, dtype) for shape, dtype in buffers]
        + [
            sem((4,)), sem((5, filts)), sem((5, filts)), sem((4,)), sem((4,)),
            sem((two_count[0],)), sem((slabs,)), sem((slabs,)), sem((two_count[0],)),
            sem((one_count[0],)), sem((slabs,)), sem((slabs,)), sem((one_count[0],)),
        ],
        compiler_params=pltpu.CompilerParams(collective_id=1, has_side_effects=True),
        name="level",
    )(x, w1, w2, og)


def on_device(volume, first_weight, second_weight, out_grad):
    w1 = first_weight.transpose(1, 4, 0, 2, 3).reshape(8, 512)
    w2 = second_weight.transpose(2, 3, 4, 1, 0).reshape(216, 128)
    result, two, one = level(volume.reshape(256, 256), w1, w2, out_grad)
    weight_two = two[:TAPS].reshape(3, 3, 3, 8, 128).transpose(4, 3, 0, 1, 2)
    one = one.reshape(2, 2, 8, 32, 2, 2).transpose(1, 3, 2, 4, 5, 0)
    weight_one = one.reshape(64, 8, 2, 2, 2)
    return (result, weight_one, weight_two)


def solution(mesh):
    in_specs = (
        P(None, "filt", "slab", None, None),
        P(None, "filt", None, None, None),
        P(None, "filt", None, None, None),
        P(None, "filt", "slab", None, None),
    )
    out_specs = (
        P(None, "filt", "slab", None, None),
        P(None, "filt", None, None, None),
        P(None, "filt", None, None, None),
    )
    return jax.shard_map(
        on_device, mesh=mesh, in_specs=in_specs, out_specs=out_specs, check_vma=False
    )
```

```python
import functools

import jax
import jax.numpy as jnp
from jax import lax
from jax.experimental import pallas as pl
from jax.experimental.pallas import tpu as pltpu
from jax.sharding import PartitionSpec as P

BF = jnp.bfloat16
F32 = jnp.float32
MESH = pl.DeviceIdType.MESH
VMEM = pl.BlockSpec(memory_space=pltpu.VMEM)
ANY = pl.BlockSpec(memory_space=pl.ANY)
TAPS = 27
W1_BLOCKS = 4


def silu_value(values):
    return values * jax.nn.sigmoid(values)


def silu_slope(values):
    logistic = jax.nn.sigmoid(values)
    return logistic * (1.0 + values * (1.0 - logistic))


def one_hot(source_of_row, size):
    row = lax.broadcasted_iota(jnp.int32, (size, size), 0)
    column = lax.broadcasted_iota(jnp.int32, (size, size), 1)
    return jnp.where(source_of_row(row) == column, 1.0, 0.0).astype(BF)


def piece_matrices():
    def source(o):
        b, d, h = o >> 7, (o >> 6) & 1, (o >> 4) & 3
        c, i, j = (o >> 2) & 3, (o >> 1) & 1, o & 1
        return (b << 7) + (c << 5) + ((2 * d + i) << 3) + 2 * h + j

    row = lax.broadcasted_iota(jnp.int32, (256, 256), 0)
    column = lax.broadcasted_iota(jnp.int32, (256, 256), 1)
    columns = jnp.where(row == 2 * (column & 127) + (column >> 7), 1.0, 0.0).astype(BF)
    return one_hot(source, 256), columns


def shifted(values, by):
    if by == 0:
        return values
    flat = values.reshape(-1, 128)
    lane = lax.broadcasted_iota(jnp.int32, flat.shape, 1)
    rolled = pltpu.roll(flat, (-by) % 128, 1)
    return jnp.where(lane == (127 if by > 0 else 0), 0.0, rolled).reshape(values.shape)


def tap(a, e, g):
    return ((a * 3 + e) * 3 + g) * 8


def nt_dot(a, b):
    return lax.dot_general(a, b, (((1,), (1,)), ((), ())), preferred_element_type=F32)


def remote(source, target, send, recv, axis, to):
    return pltpu.make_async_remote_copy(
        src_ref=source,
        dst_ref=target,
        send_sem=send,
        recv_sem=recv,
        device_id={axis: to},
        device_id_type=MESH,
    )


def repeat(low, high, step):
    lax.fori_loop(low, high, lambda i, carry: (step(i), carry)[1], 0)


class Scatter:
    def __init__(self, n, me, first, count, blocks, landing, total, out, sems):
        self.n, self.me, self.first = n, me, first
        self.owners, self.per = count
        self.blocks, self.landing, self.total, self.out = blocks, landing, total, out
        self.send_a, self.recv_a, self.send_b, self.recv_b = sems

    def owner(self, j):
        return lax.rem(self.first + j, self.n)

    def index(self):
        return lax.rem(self.me - self.first + self.n, self.n)

    def out_copy(self, j):
        return remote(
            self.blocks.at[pl.ds(j * self.per, self.per)],
            self.landing.at[self.me],
            self.send_a.at[j],
            self.recv_a.at[self.me],
            "slab",
            self.owner(j),
        )

    def in_copy(self, source):
        return remote(
            self.total,
            self.landing.at[source],
            self.send_a.at[0],
            self.recv_a.at[source],
            "slab",
            source,
        )

    def back_copy(self, r):
        at = self.index() * self.per
        return remote(
            self.total,
            self.out.at[pl.ds(at, self.per)],
            self.send_b.at[r],
            self.recv_b.at[self.index()],
            "slab",
            lax.rem(self.me + r, self.n),
        )

    def each_owner(self, step):
        def one(j):
            @pl.when(self.owner(j) != self.me)
            def _():
                step(j)

        repeat(0, self.owners, one)

    def start(self):
        self.each_owner(lambda j: self.out_copy(j).start())

    def reduce(self):
        @pl.when(self.index() < self.owners)
        def _():
            at = pl.ds(self.index() * self.per, self.per)

            def add(r, total):
                source = lax.rem(self.me + self.n - r, self.n)
                self.in_copy(source).wait_recv()
                return total + self.landing[source]

            total = lax.fori_loop(1, self.n, add, self.blocks[at])
            self.total[...] = total
            self.out[at] = total
            repeat(1, self.n, lambda r: self.back_copy(r).start())

    def finish(self):
        def arrive(j):
            remote(
                self.total,
                self.out.at[pl.ds(j * self.per, self.per)],
                self.send_b.at[0],
                self.recv_b.at[j],
                "slab",
                self.owner(j),
            ).wait_recv()

        self.each_owner(arrive)
        self.each_owner(lambda j: self.out_copy(j).wait_send())

        @pl.when(self.index() < self.owners)
        def _():
            repeat(1, self.n, lambda r: self.back_copy(r).wait_send())


def level_kernel(
    filts, slabs, two_count, one_count,
    x_hbm, w1_raw, w2_hbm, og_hbm,
    result_hbm, two_out, w1_out,
    piece, x_all, w_all, hid, y, own, up, down, below, above,
    sg, sg_below, sg_above, view, s, mid, mid_in, dw1, dw1_in, w2_t, pre_ref,
    two, two_in, two_sum, one, one_in, one_sum,
    og, res, w1_ref, w1_wide, order, x_perm, one_out, x_ref, w2_ref, og_ref, result_ref, ls, fs, fr, hs, hr, ts_a, tr_a, ts_b, tr_b, os_a, or_a, os_b, or_b,
):
    f, z = lax.axis_index("filt"), lax.axis_index("slab")
    barrier = pltpu.get_barrier_semaphore()
    loads = [
        pltpu.make_async_copy(array, place, ls.at[i])
        for i, (array, place) in enumerate(
            ((x_hbm, x_ref), (w2_hbm, w2_ref), (og_hbm, og_ref))
        )
    ]
    for copy in loads:
        copy.start()

    def greet(axis, me, n):
        def one_peer(r):
            pl.semaphore_signal(
                barrier,
                inc=1,
                device_id={axis: lax.rem(me + r, n)},
                device_id_type=MESH,
            )

        repeat(1, n, one_peer)

    greet("filt", f, filts)
    greet("slab", z, slabs)

    def other(r, sign):
        m = lax.div(r, 2)
        dy = 4 + (1 - 2 * lax.rem(m, 2)) * lax.div(m + 1, 2)
        column = lax.rem(lax.div(f, 8) + 1 + lax.rem(r, 2), 2)
        return column * 8 + lax.rem(lax.rem(f, 8) + 8 + sign * dy, 8)

    def peer(r):
        return other(r, 1)

    def source(r):
        return other(r, -1)

    def filt(i, r, block, target):
        return remote(block, target, fs.at[i, r], fr.at[i, r], "filt", peer(r))

    def to_all(step):
        repeat(0, filts - 1, step)

    def from_all(step, start):
        return lax.fori_loop(
            0, filts - 1, lambda r, carry: step(filts - 2 - r, carry), start
        )

    rows, columns = piece_matrices()
    loads[0].wait()
    half = jnp.dot(rows, x_ref[...], preferred_element_type=F32).astype(BF)
    cut = jnp.dot(half, columns, preferred_element_type=F32).astype(BF)
    piece[...] = cut.reshape(piece.shape)
    x_all[f] = piece[f]
    for n in range(8):
        for t in range(4):
            both = w1_raw[n, t].astype(F32)
            for k in range(2):
                w1_wide[k * 4 + t, n : n + 1, :] = both[k : k + 1, :]
    for t in range(8):
        w1_ref[:, t * 64 : (t + 1) * 64] = w1_wide[t].astype(BF)
    w_all[f] = w1_ref[...]
    pl.semaphore_wait(barrier, filts + slabs - 2)

    def send_x(r):
        filt(0, r, piece.at[peer(r)], x_all.at[f]).start()
        filt(1, r, w1_ref, w_all.at[f]).start()

    to_all(send_x)
    order[...] = one_hot(lambda o: ((o & 63) << 2) + (o >> 6), 256)
    loads[1].wait()
    loads[2].wait()
    for b in range(2):
        for d in range(2):
            for n in range(8):
                og[d, b, :, n, :] = og_ref[b, n, d].astype(F32)
    eye = one_hot(lambda o: o, 128)
    w2_t[...] = nt_dot(eye, w2_ref[...]).astype(BF)
    y[:, :, 0] = jnp.zeros((2, 2, 216, 128), F32)
    y[:, :, 5] = jnp.zeros((2, 2, 216, 128), F32)
    view[:, :, :, 0] = jnp.zeros((3, 2, 4, 8, 128), F32)
    view[:, :, :, 5] = jnp.zeros((3, 2, 4, 8, 128), F32)

    def get_x(r):
        filt(0, r, piece.at[peer(r)], x_all.at[source(r)]).wait_recv()
        filt(1, r, w1_ref, w_all.at[source(r)]).wait_recv()

    to_all(get_x)
    x = x_all[...].reshape(256, 256)
    x = jnp.dot(order[...], x, preferred_element_type=F32).astype(BF)
    x_perm[...] = x
    w = w_all[...].reshape(128, 512)
    pre = jnp.dot(w[:, :256], x[:, :128], preferred_element_type=F32)
    pre += jnp.dot(w[:, 256:], x[:, 128:], preferred_element_type=F32)
    pre_ref[...] = pre
    hid[f] = silu_value(pre).astype(BF)
    to_all(lambda r: filt(2, r, hid.at[f], hid.at[f]).start())

    def spread(q):
        b, d, h = lax.div(q, 8), lax.rem(lax.div(q, 4), 2), lax.rem(q, 4)
        y[b, d, h + 1] = jnp.dot(w2_ref[...], hid[q], preferred_element_type=F32)

    spread(f)

    def get_hidden(r):
        filt(2, r, hid.at[f], hid.at[source(r)]).wait_recv()
        spread(source(r))

    from_all(lambda r, carry: (get_hidden(r), carry)[1], 0)
    for d in (-1, 2, 0, 1):
        total = None
        for g in range(3):
            part = None
            for a in range(3):
                plane = d + a - 1
                if plane < 0 or plane > 1:
                    continue
                for e in range(3):
                    at = tap(a, e, g)
                    term = y[:, plane, e : e + 4, at : at + 8, :]
                    part = term if part is None else part + term
            part = shifted(part, g - 1)
            total = part if total is None else total + part
        if d < 0:
            down[...] = total
        elif d > 1:
            up[...] = total
        else:
            own[d] = total

    after, before = lax.rem(z + 1, slabs), lax.rem(z + slabs - 1, slabs)

    def rims(i, block_up, block_down, from_below, from_above):
        return (
            remote(block_up, from_below, hs.at[i], hr.at[i], "slab", after),
            remote(block_down, from_above, hs.at[i + 1], hr.at[i + 1], "slab", before),
        )

    first_rims = rims(0, up, down, below, above)
    for copy in first_rims:
        copy.start()
    inside = (z > 0, z < slabs - 1)
    for copy in first_rims:
        copy.wait_recv()
    for d in range(2):
        rim = (below if d == 0 else above)[...]
        second_pre = own[d] + jnp.where(inside[d], rim, 0.0)
        res[d] = silu_value(second_pre)
        grad = og[d] * silu_slope(second_pre)
        sg[d] = grad.astype(BF)
    second_rims = rims(2, sg.at[1], sg.at[0], sg_below, sg_above)
    for copy in second_rims:
        copy.start()

    def put_view(plane, values):
        for g in range(3):
            view[g, :, plane + 1, 1:5] = shifted(values, 1 - g)

    for d in range(2):
        put_view(d, sg[d].astype(F32))
        for b in range(2):
            for n in range(8):
                result_ref[b, n, d] = res[d, b, :, n, :].astype(BF)

    def put_taps(d, a):
        for e in range(3):
            for g in range(3):
                at = tap(a, e, g)
                s[:, d, :, at : at + 8, :] = view[g, :, d - a + 2, 2 - e : 6 - e]

    for d in range(2):
        put_taps(d, 1)
        put_taps(d, 2 * d)
    for copy in second_rims:
        copy.wait_recv()
    put_view(-1, jnp.where(inside[0], sg_below[...].astype(F32), 0.0))
    put_view(2, jnp.where(inside[1], sg_above[...].astype(F32), 0.0))
    for d in range(2):
        put_taps(d, 2 - 2 * d)

    def taps_of(q):
        b, d, h = lax.div(q, 8), lax.rem(lax.div(q, 4), 2), lax.rem(q, 4)
        return s[b, d, h].astype(BF)

    def back(q):
        part = jnp.dot(w2_t[...], taps_of(q), preferred_element_type=F32)
        mid[q] = part.astype(BF)

    def send_mid(r):
        filt(3, r, mid.at[peer(r)], mid_in.at[f]).start()

    back(peer(0))

    def back_step(r):
        back(peer(r))
        send_mid(r - 1)

    repeat(1, filts - 1, back_step)
    back(f)
    send_mid(filts - 2)
    total = lax.fori_loop(
        0,
        filts,
        lambda q, total: total + nt_dot(taps_of(q), hid[q]),
        jnp.zeros((216, 128), F32),
    )
    store = pltpu.make_async_copy(result_ref, result_hbm, ls.at[3])
    store.start()
    two[:TAPS] = total.reshape(TAPS, 8, 128)
    two_sums = Scatter(
        slabs, z, 0, two_count, two, two_in, two_sum, two_out, (ts_a, tr_a, ts_b, tr_b)
    )
    two_sums.start()

    def get_mid(r, total):
        filt(3, r, mid.at[peer(r)], mid_in.at[source(r)]).wait_recv()
        return total + mid_in[source(r)].astype(F32)

    mid_grad = from_all(get_mid, mid[f].astype(F32))
    grad = (mid_grad * silu_slope(pre_ref[...])).astype(BF)
    x = x_perm[...]
    for k in range(2):
        part = nt_dot(grad, x[:, k * 128 : (k + 1) * 128])
        dw1[:, :, k * 256 : (k + 1) * 256] = part.reshape(16, 8, 256).astype(BF)
    to_all(lambda r: filt(4, r, dw1.at[peer(r)], dw1_in.at[f]).start())
    two_sums.reduce()

    def get_one(r, total):
        filt(4, r, dw1.at[peer(r)], dw1_in.at[source(r)]).wait_recv()
        return total + dw1_in[source(r)].astype(F32)

    first = from_all(get_one, dw1[f].astype(F32))
    for j in range(W1_BLOCKS):
        one[j] = first[:, j * 128 : (j + 1) * 128]
    one_first = TAPS if slabs >= TAPS + W1_BLOCKS else 0
    one_sums = Scatter(
        slabs, z, one_first, one_count, one, one_in, one_sum, one_out,
        (os_a, or_a, os_b, or_b),
    )
    one_sums.start()

    def sent(r):
        filt(0, r, piece.at[peer(r)], x_all.at[f]).wait_send()
        filt(1, r, w1_ref, w_all.at[f]).wait_send()
        filt(2, r, hid.at[f], hid.at[f]).wait_send()
        filt(3, r, mid.at[peer(r)], mid_in.at[f]).wait_send()
        filt(4, r, dw1.at[peer(r)], dw1_in.at[f]).wait_send()

    to_all(sent)
    for copy in first_rims + second_rims:
        copy.wait_send()
    one_sums.reduce()
    two_sums.finish()
    one_sums.finish()
    for j in range(W1_BLOCKS):
        for t in range(2):
            w1_out[:, j % 2 * 2 + t, j // 2, :] = one_out[j][:, t * 64 : (t + 1) * 64]
    store.wait()


def owners(blocks, n):
    per = -(-blocks // n)
    return -(-blocks // per), per


def level(x, w1, w2, og):
    filts, slabs = lax.axis_size("filt"), lax.axis_size("slab")
    two_count, one_count = owners(TAPS, slabs), owners(W1_BLOCKS, slabs)
    two_size, one_size = (c[0] * c[1] for c in (two_count, one_count))
    sem = pltpu.SemaphoreType.DMA
    buffers = [
        ((16, 16, 256), BF), ((16, 16, 256), BF), ((16, 8, 512), BF),
        ((16, 128, 128), BF), ((2, 2, 6, 216, 128), F32), ((2, 2, 4, 8, 128), F32),
        ((2, 4, 8, 128), F32), ((2, 4, 8, 128), F32),
        ((2, 4, 8, 128), F32), ((2, 4, 8, 128), F32),
        ((2, 2, 4, 8, 128), BF), ((2, 4, 8, 128), BF), ((2, 4, 8, 128), BF),
        ((3, 2, 4, 6, 8, 128), F32), ((2, 2, 4, 216, 128), F32),
        ((16, 128, 128), BF), ((16, 128, 128), BF),
        ((16, 8, 512), BF), ((16, 8, 512), BF), ((128, 216), BF), ((128, 128), F32),
        ((two_size, 8, 128), F32), ((slabs, two_count[1], 8, 128), F32),
        ((two_count[1], 8, 128), F32),
        ((one_size, 8, 128), F32), ((slabs, one_count[1], 8, 128), F32),
        ((one_count[1], 8, 128), F32),
        ((2, 2, 4, 8, 128), F32), ((2, 2, 4, 8, 128), F32),
        ((8, 512), BF), ((8, 8, 64), F32), ((256, 256), BF), ((256, 256), BF),
        ((one_size, 8, 128), F32),
        ((256, 256), BF), ((216, 128), BF), ((2, 8, 2, 4, 128), BF),
        ((2, 8, 2, 4, 128), BF),
    ]
    return pl.pallas_call(
        functools.partial(level_kernel, filts, slabs, two_count, one_count),
        out_shape=[
            jax.ShapeDtypeStruct((2, 8, 2, 4, 128), BF),
            jax.ShapeDtypeStruct((two_size, 8, 128), F32),
            jax.ShapeDtypeStruct((8, 4, 2, 64), F32),
        ],
        in_specs=[ANY, VMEM, ANY, ANY],
        out_specs=[ANY, VMEM, VMEM],
        scratch_shapes=[pltpu.VMEM(shape, dtype) for shape, dtype in buffers]
        + [
            sem((4,)), sem((5, filts)), sem((5, filts)), sem((4,)), sem((4,)),
            sem((two_count[0],)), sem((slabs,)), sem((slabs,)), sem((two_count[0],)),
            sem((one_count[0],)), sem((slabs,)), sem((slabs,)), sem((one_count[0],)),
        ],
        compiler_params=pltpu.CompilerParams(collective_id=1, has_side_effects=True),
        name="level",
    )(x, w1, w2, og)


def on_device(volume, first_weight, second_weight, out_grad):
    w1 = first_weight.transpose(1, 2, 3, 4, 0).reshape(8, 4, 2, 64)
    w2 = second_weight.transpose(2, 3, 4, 1, 0).reshape(216, 128)
    result, two, one = level(volume.reshape(256, 256), w1, w2, out_grad)
    weight_two = two[:TAPS].reshape(3, 3, 3, 8, 128).transpose(4, 3, 0, 1, 2)
    weight_one = one.reshape(8, 2, 2, 2, 64).transpose(4, 0, 1, 2, 3)
    return (result, weight_one, weight_two)


def solution(mesh):
    in_specs = (
        P(None, "filt", "slab", None, None),
        P(None, "filt", None, None, None),
        P(None, "filt", None, None, None),
        P(None, "filt", "slab", None, None),
    )
    out_specs = (
        P(None, "filt", "slab", None, None),
        P(None, "filt", None, None, None),
        P(None, "filt", None, None, None),
    )
    return jax.shard_map(
        on_device, mesh=mesh, in_specs=in_specs, out_specs=out_specs, check_vma=False
    )
```

```python
import functools

import jax
import jax.numpy as jnp
from jax import lax
from jax.experimental import pallas as pl
from jax.experimental.pallas import tpu as pltpu
from jax.sharding import PartitionSpec as P

BF = jnp.bfloat16
F32 = jnp.float32
MESH = pl.DeviceIdType.MESH
VMEM = pl.BlockSpec(memory_space=pltpu.VMEM)
ANY = pl.BlockSpec(memory_space=pl.ANY)
TAPS = 27
W1_BLOCKS = 4


def silu_value(values):
    return values * jax.nn.sigmoid(values)


def silu_slope(values):
    logistic = jax.nn.sigmoid(values)
    return logistic * (1.0 + values * (1.0 - logistic))


def one_hot(source_of_row, size):
    row = lax.broadcasted_iota(jnp.int32, (size, size), 0)
    column = lax.broadcasted_iota(jnp.int32, (size, size), 1)
    return jnp.where(source_of_row(row) == column, 1.0, 0.0).astype(BF)


def piece_matrices():
    def source(o):
        b, d, h = o >> 7, (o >> 6) & 1, (o >> 4) & 3
        c, i, j = (o >> 2) & 3, (o >> 1) & 1, o & 1
        return (b << 7) + (c << 5) + ((2 * d + i) << 3) + 2 * h + j

    row = lax.broadcasted_iota(jnp.int32, (256, 256), 0)
    column = lax.broadcasted_iota(jnp.int32, (256, 256), 1)
    columns = jnp.where(row == 2 * (column & 127) + (column >> 7), 1.0, 0.0).astype(BF)
    return one_hot(source, 256), columns


def shifted(values, by):
    if by == 0:
        return values
    flat = values.reshape(-1, 128)
    lane = lax.broadcasted_iota(jnp.int32, flat.shape, 1)
    rolled = pltpu.roll(flat, (-by) % 128, 1)
    return jnp.where(lane == (127 if by > 0 else 0), 0.0, rolled).reshape(values.shape)


def tap(a, e, g):
    return ((a * 3 + e) * 3 + g) * 8


def nt_dot(a, b):
    return lax.dot_general(a, b, (((1,), (1,)), ((), ())), preferred_element_type=F32)


def remote(source, target, send, recv, axis, to):
    return pltpu.make_async_remote_copy(
        src_ref=source,
        dst_ref=target,
        send_sem=send,
        recv_sem=recv,
        device_id={axis: to},
        device_id_type=MESH,
    )


def repeat(low, high, step):
    lax.fori_loop(low, high, lambda i, carry: (step(i), carry)[1], 0)


class Scatter:
    def __init__(self, n, me, first, count, blocks, landing, total, out, sems):
        self.n, self.me, self.first = n, me, first
        self.owners, self.per = count
        self.blocks, self.landing, self.total, self.out = blocks, landing, total, out
        self.send_a, self.recv_a, self.send_b, self.recv_b = sems

    def owner(self, j):
        return lax.rem(self.first + j, self.n)

    def index(self):
        return lax.rem(self.me - self.first + self.n, self.n)

    def out_copy(self, j):
        return remote(
            self.blocks.at[pl.ds(j * self.per, self.per)],
            self.landing.at[self.me],
            self.send_a.at[j],
            self.recv_a.at[self.me],
            "slab",
            self.owner(j),
        )

    def in_copy(self, source):
        return remote(
            self.total,
            self.landing.at[source],
            self.send_a.at[0],
            self.recv_a.at[source],
            "slab",
            source,
        )

    def back_copy(self, r):
        at = self.index() * self.per
        return remote(
            self.total,
            self.out.at[pl.ds(at, self.per)],
            self.send_b.at[r],
            self.recv_b.at[self.index()],
            "slab",
            lax.rem(self.me + r, self.n),
        )

    def each_owner(self, step):
        def one(j):
            @pl.when(self.owner(j) != self.me)
            def _():
                step(j)

        repeat(0, self.owners, one)

    def start(self):
        self.each_owner(lambda j: self.out_copy(j).start())

    def reduce(self):
        @pl.when(self.index() < self.owners)
        def _():
            at = pl.ds(self.index() * self.per, self.per)

            def add(r, total):
                source = lax.rem(self.me + self.n - r, self.n)
                self.in_copy(source).wait_recv()
                return total + self.landing[source]

            total = lax.fori_loop(1, self.n, add, self.blocks[at])
            self.total[...] = total
            self.out[at] = total
            repeat(1, self.n, lambda r: self.back_copy(r).start())

    def finish(self):
        def arrive(j):
            remote(
                self.total,
                self.out.at[pl.ds(j * self.per, self.per)],
                self.send_b.at[0],
                self.recv_b.at[j],
                "slab",
                self.owner(j),
            ).wait_recv()

        self.each_owner(arrive)
        self.each_owner(lambda j: self.out_copy(j).wait_send())

        @pl.when(self.index() < self.owners)
        def _():
            repeat(1, self.n, lambda r: self.back_copy(r).wait_send())


def level_kernel(
    filts, slabs, two_count, one_count,
    x_hbm, w1_raw, w2_hbm, og_hbm,
    result_hbm, two_out, w1_out,
    piece, x_all, w_all, hid, y, own, up, down, below, above,
    sg, sg_below, sg_above, view, s, mid, mid_in, dw1, dw1_in, w2_t, pre_ref,
    two, two_in, two_sum, one, one_in, one_sum,
    og, res, w1_ref, w1_wide, order, x_perm, one_out, x_ref, w2_ref, og_ref, result_ref, ls, fs, fr, hs, hr, ts_a, tr_a, ts_b, tr_b, os_a, or_a, os_b, or_b,
):
    f, z = lax.axis_index("filt"), lax.axis_index("slab")
    barrier = pltpu.get_barrier_semaphore()
    loads = [
        pltpu.make_async_copy(array, place, ls.at[i])
        for i, (array, place) in enumerate(
            ((x_hbm, x_ref), (w2_hbm, w2_ref), (og_hbm, og_ref))
        )
    ]
    for copy in loads:
        copy.start()

    def greet(axis, me, n):
        def one_peer(r):
            pl.semaphore_signal(
                barrier,
                inc=1,
                device_id={axis: lax.rem(me + r, n)},
                device_id_type=MESH,
            )

        repeat(1, n, one_peer)

    greet("filt", f, filts)
    greet("slab", z, slabs)

    def other(r, sign):
        m = lax.div(r, 2)
        dy = 4 + (1 - 2 * lax.rem(m, 2)) * lax.div(m + 1, 2)
        column = lax.rem(lax.div(f, 8) + 1 + lax.rem(r, 2), 2)
        return column * 8 + lax.rem(lax.rem(f, 8) + 8 + sign * dy, 8)

    def peer(r):
        return other(r, 1)

    def source(r):
        return other(r, -1)

    def filt(i, r, block, target):
        return remote(block, target, fs.at[i, r], fr.at[i, r], "filt", peer(r))

    def to_all(step):
        repeat(0, filts - 1, step)

    def from_all(step, start):
        return lax.fori_loop(
            0, filts - 1, lambda r, carry: step(filts - 2 - r, carry), start
        )

    rows, columns = piece_matrices()
    loads[0].wait()
    half = jnp.dot(rows, x_ref[...], preferred_element_type=F32).astype(BF)
    cut = jnp.dot(half, columns, preferred_element_type=F32).astype(BF)
    piece[...] = cut.reshape(piece.shape)
    x_all[f] = piece[f]
    for n in range(8):
        for t in range(4):
            both = w1_raw[n, t].astype(F32)
            for k in range(2):
                w1_wide[k * 4 + t, n : n + 1, :] = both[k : k + 1, :]
    for t in range(8):
        w1_ref[:, t * 64 : (t + 1) * 64] = w1_wide[t].astype(BF)
    w_all[f] = w1_ref[...]
    pl.semaphore_wait(barrier, filts + slabs - 2)

    def send_x(r):
        filt(0, r, piece.at[peer(r)], x_all.at[f]).start()
        filt(1, r, w1_ref, w_all.at[f]).start()

    to_all(send_x)
    order[...] = one_hot(lambda o: ((o & 63) << 2) + (o >> 6), 256)
    loads[1].wait()
    loads[2].wait()
    for b in range(2):
        for d in range(2):
            for n in range(8):
                og[d, b, :, n, :] = og_ref[b, n, d].astype(F32)
    eye = one_hot(lambda o: o, 128)
    w2_t[...] = nt_dot(eye, w2_ref[...]).astype(BF)
    y[:, :, 0] = jnp.zeros((2, 2, 216, 128), F32)
    y[:, :, 5] = jnp.zeros((2, 2, 216, 128), F32)
    view[:, :, :, 0] = jnp.zeros((3, 2, 4, 8, 128), F32)
    view[:, :, :, 5] = jnp.zeros((3, 2, 4, 8, 128), F32)

    def get_x(r):
        filt(0, r, piece.at[peer(r)], x_all.at[source(r)]).wait_recv()
        filt(1, r, w1_ref, w_all.at[source(r)]).wait_recv()

    to_all(get_x)
    x = x_all[...].reshape(256, 256)
    x = jnp.dot(order[...], x, preferred_element_type=F32).astype(BF)
    x_perm[...] = x
    w = w_all[...].reshape(128, 512)
    pre = jnp.dot(w[:, :256], x[:, :128], preferred_element_type=F32)
    pre += jnp.dot(w[:, 256:], x[:, 128:], preferred_element_type=F32)
    pre_ref[...] = pre
    hid[f] = silu_value(pre).astype(BF)
    to_all(lambda r: filt(2, r, hid.at[f], hid.at[f]).start())

    def spread(q):
        b, d, h = lax.div(q, 8), lax.rem(lax.div(q, 4), 2), lax.rem(q, 4)
        y[b, d, h + 1] = jnp.dot(w2_ref[...], hid[q], preferred_element_type=F32)

    spread(f)

    def get_hidden(r):
        filt(2, r, hid.at[f], hid.at[source(r)]).wait_recv()
        spread(source(r))

    from_all(lambda r, carry: (get_hidden(r), carry)[1], 0)
    def stencil(d):
        total = None
        for g in range(3):
            part = None
            for a in range(3):
                plane = d + a - 1
                if plane < 0 or plane > 1:
                    continue
                for e in range(3):
                    at = tap(a, e, g)
                    term = y[:, plane, e : e + 4, at : at + 8, :]
                    part = term if part is None else part + term
            part = shifted(part, g - 1)
            total = part if total is None else total + part
        if d < 0:
            down[...] = total
        elif d > 1:
            up[...] = total
        else:
            own[d] = total

    stencil(-1)
    stencil(2)
    after, before = lax.rem(z + 1, slabs), lax.rem(z + slabs - 1, slabs)

    def rims(i, block_up, block_down, from_below, from_above):
        return (
            remote(block_up, from_below, hs.at[i], hr.at[i], "slab", after),
            remote(block_down, from_above, hs.at[i + 1], hr.at[i + 1], "slab", before),
        )

    first_rims = rims(0, up, down, below, above)
    for copy in first_rims:
        copy.start()
    stencil(0)
    stencil(1)
    inside = (z > 0, z < slabs - 1)
    for copy in first_rims:
        copy.wait_recv()
    for d in range(2):
        rim = (below if d == 0 else above)[...]
        second_pre = own[d] + jnp.where(inside[d], rim, 0.0)
        res[d] = silu_value(second_pre)
        grad = og[d] * silu_slope(second_pre)
        sg[d] = grad.astype(BF)
    second_rims = rims(2, sg.at[1], sg.at[0], sg_below, sg_above)
    for copy in second_rims:
        copy.start()

    def put_view(plane, values):
        for g in range(3):
            view[g, :, plane + 1, 1:5] = shifted(values, 1 - g)

    for d in range(2):
        put_view(d, sg[d].astype(F32))
        for b in range(2):
            for n in range(8):
                result_ref[b, n, d] = res[d, b, :, n, :].astype(BF)

    def put_taps(d, a):
        for e in range(3):
            for g in range(3):
                at = tap(a, e, g)
                s[:, d, :, at : at + 8, :] = view[g, :, d - a + 2, 2 - e : 6 - e]

    for d in range(2):
        put_taps(d, 1)
        put_taps(d, 2 * d)
    for copy in second_rims:
        copy.wait_recv()
    put_view(-1, jnp.where(inside[0], sg_below[...].astype(F32), 0.0))
    put_view(2, jnp.where(inside[1], sg_above[...].astype(F32), 0.0))
    for d in range(2):
        put_taps(d, 2 - 2 * d)

    def taps_of(q):
        b, d, h = lax.div(q, 8), lax.rem(lax.div(q, 4), 2), lax.rem(q, 4)
        return s[b, d, h].astype(BF)

    def back(q):
        part = jnp.dot(w2_t[...], taps_of(q), preferred_element_type=F32)
        mid[q] = part.astype(BF)

    def send_mid(r):
        filt(3, r, mid.at[peer(r)], mid_in.at[f]).start()

    back(peer(0))

    def back_step(r):
        back(peer(r))
        send_mid(r - 1)

    repeat(1, filts - 1, back_step)
    back(f)
    send_mid(filts - 2)
    total = lax.fori_loop(
        0,
        filts,
        lambda q, total: total + nt_dot(taps_of(q), hid[q]),
        jnp.zeros((216, 128), F32),
    )
    store = pltpu.make_async_copy(result_ref, result_hbm, ls.at[3])
    store.start()
    two[:TAPS] = total.reshape(TAPS, 8, 128)
    two_sums = Scatter(
        slabs, z, 0, two_count, two, two_in, two_sum, two_out, (ts_a, tr_a, ts_b, tr_b)
    )
    two_sums.start()

    def get_mid(r, total):
        filt(3, r, mid.at[peer(r)], mid_in.at[source(r)]).wait_recv()
        return total + mid_in[source(r)].astype(F32)

    mid_grad = from_all(get_mid, mid[f].astype(F32))
    grad = (mid_grad * silu_slope(pre_ref[...])).astype(BF)
    x = x_perm[...]
    for k in range(2):
        part = nt_dot(grad, x[:, k * 128 : (k + 1) * 128])
        dw1[:, :, k * 256 : (k + 1) * 256] = part.reshape(16, 8, 256).astype(BF)
    to_all(lambda r: filt(4, r, dw1.at[peer(r)], dw1_in.at[f]).start())
    two_sums.reduce()

    def get_one(r, total):
        filt(4, r, dw1.at[peer(r)], dw1_in.at[source(r)]).wait_recv()
        return total + dw1_in[source(r)].astype(F32)

    first = from_all(get_one, dw1[f].astype(F32))
    for j in range(W1_BLOCKS):
        one[j] = first[:, j * 128 : (j + 1) * 128]
    one_first = TAPS if slabs >= TAPS + W1_BLOCKS else 0
    one_sums = Scatter(
        slabs, z, one_first, one_count, one, one_in, one_sum, one_out,
        (os_a, or_a, os_b, or_b),
    )
    one_sums.start()

    def sent(r):
        filt(0, r, piece.at[peer(r)], x_all.at[f]).wait_send()
        filt(1, r, w1_ref, w_all.at[f]).wait_send()
        filt(2, r, hid.at[f], hid.at[f]).wait_send()
        filt(3, r, mid.at[peer(r)], mid_in.at[f]).wait_send()
        filt(4, r, dw1.at[peer(r)], dw1_in.at[f]).wait_send()

    to_all(sent)
    for copy in first_rims + second_rims:
        copy.wait_send()
    one_sums.reduce()
    two_sums.finish()
    one_sums.finish()
    for j in range(W1_BLOCKS):
        for t in range(2):
            w1_out[:, j % 2 * 2 + t, j // 2, :] = one_out[j][:, t * 64 : (t + 1) * 64]
    store.wait()


def owners(blocks, n):
    per = -(-blocks // n)
    return -(-blocks // per), per


def level(x, w1, w2, og):
    filts, slabs = lax.axis_size("filt"), lax.axis_size("slab")
    two_count, one_count = owners(TAPS, slabs), owners(W1_BLOCKS, slabs)
    two_size, one_size = (c[0] * c[1] for c in (two_count, one_count))
    sem = pltpu.SemaphoreType.DMA
    buffers = [
        ((16, 16, 256), BF), ((16, 16, 256), BF), ((16, 8, 512), BF),
        ((16, 128, 128), BF), ((2, 2, 6, 216, 128), F32), ((2, 2, 4, 8, 128), F32),
        ((2, 4, 8, 128), F32), ((2, 4, 8, 128), F32),
        ((2, 4, 8, 128), F32), ((2, 4, 8, 128), F32),
        ((2, 2, 4, 8, 128), BF), ((2, 4, 8, 128), BF), ((2, 4, 8, 128), BF),
        ((3, 2, 4, 6, 8, 128), F32), ((2, 2, 4, 216, 128), F32),
        ((16, 128, 128), BF), ((16, 128, 128), BF),
        ((16, 8, 512), BF), ((16, 8, 512), BF), ((128, 216), BF), ((128, 128), F32),
        ((two_size, 8, 128), F32), ((slabs, two_count[1], 8, 128), F32),
        ((two_count[1], 8, 128), F32),
        ((one_size, 8, 128), F32), ((slabs, one_count[1], 8, 128), F32),
        ((one_count[1], 8, 128), F32),
        ((2, 2, 4, 8, 128), F32), ((2, 2, 4, 8, 128), F32),
        ((8, 512), BF), ((8, 8, 64), F32), ((256, 256), BF), ((256, 256), BF),
        ((one_size, 8, 128), F32),
        ((256, 256), BF), ((216, 128), BF), ((2, 8, 2, 4, 128), BF),
        ((2, 8, 2, 4, 128), BF),
    ]
    return pl.pallas_call(
        functools.partial(level_kernel, filts, slabs, two_count, one_count),
        out_shape=[
            jax.ShapeDtypeStruct((2, 8, 2, 4, 128), BF),
            jax.ShapeDtypeStruct((two_size, 8, 128), F32),
            jax.ShapeDtypeStruct((8, 4, 2, 64), F32),
        ],
        in_specs=[ANY, VMEM, ANY, ANY],
        out_specs=[ANY, VMEM, VMEM],
        scratch_shapes=[pltpu.VMEM(shape, dtype) for shape, dtype in buffers]
        + [
            sem((4,)), sem((5, filts)), sem((5, filts)), sem((4,)), sem((4,)),
            sem((two_count[0],)), sem((slabs,)), sem((slabs,)), sem((two_count[0],)),
            sem((one_count[0],)), sem((slabs,)), sem((slabs,)), sem((one_count[0],)),
        ],
        compiler_params=pltpu.CompilerParams(collective_id=1, has_side_effects=True),
        name="level",
    )(x, w1, w2, og)


def on_device(volume, first_weight, second_weight, out_grad):
    w1 = first_weight.transpose(1, 2, 3, 4, 0).reshape(8, 4, 2, 64)
    w2 = second_weight.transpose(2, 3, 4, 1, 0).reshape(216, 128)
    result, two, one = level(volume.reshape(256, 256), w1, w2, out_grad)
    weight_two = two[:TAPS].reshape(3, 3, 3, 8, 128).transpose(4, 3, 0, 1, 2)
    weight_one = one.reshape(8, 2, 2, 2, 64).transpose(4, 0, 1, 2, 3)
    return (result, weight_one, weight_two)


def solution(mesh):
    in_specs = (
        P(None, "filt", "slab", None, None),
        P(None, "filt", None, None, None),
        P(None, "filt", None, None, None),
        P(None, "filt", "slab", None, None),
    )
    out_specs = (
        P(None, "filt", "slab", None, None),
        P(None, "filt", None, None, None),
        P(None, "filt", None, None, None),
    )
    return jax.shard_map(
        on_device, mesh=mesh, in_specs=in_specs, out_specs=out_specs, check_vma=False
    )
```
